128 devices in a mesh: seq: 32 (over x_hi, y, z), head: 4 (over x_lo, core).
Axes of the slice: x: 4 (x_hi: 2, x_lo: 2; x = x_hi * 2 + x_lo), y: 4, z: 4, core: 2. Of those that a mesh axis runs over, the one named last changes fastest.
Arguments:
- queries: bfloat16 [16384, 5120], P(('seq', 'head')), may hold values from -163 to 163
- keys: bfloat16 [16384, 5120], P(('seq', 'head')), may hold values from -6.5 to 6.5
- values: bfloat16 [16384, 5120], P(('seq', 'head')), may hold values from -6 to 6
- step_rate: bfloat16 [16384, 8], P(('seq', 'head')), may hold values from 0.099609375 to 1
- doc_start: int32 [16384], P('seq'), may hold values from 0 to 16383, as said below
- window_len: int32 [40], replicated, may hold values from 512 to 2048, as said below
- head_order: int32 [40], replicated, may hold values from 0 to 39, each once
- learn_rate: float32 [8], replicated, may hold values from 0.01 to 0.04
- w_gate: bfloat16 [8, 640, 640], P('head'), may hold values from -0.25 to 0.25
- w_up: bfloat16 [8, 640, 640], P('head'), may hold values from -0.25 to 0.25
- w_down: bfloat16 [8, 640, 640], P('head'), may hold values from -0.25 to 0.25
Outputs:
- mixed: bfloat16 [16384, 5120], P(('seq', 'head'))
The draws below stay inside these ranges and needn't reach their ends.
Inputs may be any that keep to these rules, and one draw needn't show every extreme that they name: doc_start[t] is the first position of the document holding t: at most t, never falling, equal to t where a document begins; a document begins at position 16383. `window_len`: some head has a window of exactly 2048. `head_order`: a permutation of the 40 heads.
All inputs are finite; a program needn't handle non-finite values.
Results may differ from the reference program's by a relative error of at most 0.03.
Values may be sent and summed in bfloat16 or wider, within the bound.
A program may use at most 128 MiB of HBM per device.

```python
import math
import jax
import jax.numpy as jnp
from jax import lax

HEADS = 40
HD = 128
FAST = 8
FH = 640
WINDOW = 2048
TOK_DEV = 128
D = 5120
FW = 640
TOKENS = 16384
N_HEAD = 4


def pair_draw(key):
    base = jax.random.fold_in(key, 11)
    key_query, key_keys = jax.random.split(base, 2)
    keys_f = jnp.clip(jax.random.normal(key_keys, (TOKENS, D), jnp.float32), -6.0, 6.0)
    queries_f = 1.5 * jnp.clip(jax.random.normal(key_query, (TOKENS, D), jnp.float32), -6.0, 6.0)
    return (queries_f, keys_f)


def draw_queries(key, part):
    return pair_draw(key)[0].astype(jnp.bfloat16)


def draw_keys(key, part):
    return pair_draw(key)[1].astype(jnp.bfloat16)


def draw_window_len(key, part):
    key_width, key_chosen = jax.random.split(jax.random.fold_in(key, 3))
    widths = jax.random.randint(key_width, (HEADS,), WINDOW // 4, WINDOW + 1)
    chosen = jax.random.randint(key_chosen, (), 0, HEADS)
    return jnp.where(jnp.arange(HEADS, dtype=jnp.int32) == chosen, WINDOW, widths).astype(jnp.int32)


def draw_doc_start(key, part):
    position = jnp.arange(TOKENS, dtype=jnp.int32)
    marked = (jax.random.randint(jax.random.fold_in(key, 5), (TOKENS,), 0, 2 * TOK_DEV * N_HEAD) == 0) | (position == 0) | (position == TOKENS - 1)
    return lax.cummax(jnp.where(marked, position, 0), axis=0).astype(jnp.int32)


def level_of(own_key, extent, cuts, least, high):
    def one(dim, shards_of):
        heights = jax.random.uniform(jax.random.fold_in(jax.random.fold_in(own_key, 6), dim), (shards_of,), jnp.float32, least / len(cuts), high / len(cuts))
        return jnp.repeat(jnp.exp(heights), extent[dim] // shards_of).reshape((-1,) + (1,) * (len(extent) - dim - 1))

    level = one(*cuts[0])
    for cut in cuts[1:]:
        level = level * one(*cut)
    return level


def scatter_about(stream_key, dims, scale, most, cuts=(), kind=jnp.bfloat16):
    loudness = level_of(stream_key, dims, cuts, -0.22, 0.18) if cuts else 1.0
    values = jax.random.normal(stream_key, dims, jnp.float32) * scale * loudness
    return jnp.minimum(jnp.maximum(values, -most), most).astype(kind)


def setup_inputs(seed: int = 0) -> dict:
    key_of = jax.random.split(jax.random.key(seed), 12)
    return {
        "queries": draw_queries(jax.random.fold_in(key_of[11], 71), 0),
        "keys": draw_keys(jax.random.fold_in(key_of[11], 71), 0),
        "values": scatter_about(key_of[2], (TOKENS, D), 1.0, 6.0, ((0, 128),)),
        "step_rate": jnp.clip(jnp.exp(math.log(1.0) - 2.306499 * jax.random.uniform(key_of[3], (TOKENS, FAST), jnp.float32) ** level_of(key_of[3], (TOKENS, FAST), ((0, 128),), -0.2, 0.2)), 0.099609375, 1.0).astype(jnp.bfloat16),
        "doc_start": draw_doc_start(jax.random.fold_in(key_of[11], 71), 0),
        "window_len": draw_window_len(jax.random.fold_in(key_of[11], 71), 0),
        "head_order": jax.random.permutation(key_of[6], HEADS).astype(jnp.int32),
        "learn_rate": jnp.clip(jnp.exp(jax.random.uniform(key_of[7], (FAST,), jnp.float32, math.log(0.01), math.log(0.04))), 0.01, 0.04),
        "w_gate": scatter_about(key_of[8], (FAST, FW, FH), FW ** -0.5, 0.25, ((0, 4),)),
        "w_up": scatter_about(key_of[9], (FAST, FW, FH), FW ** -0.5, 0.25, ((0, 4),)),
        "w_down": scatter_about(key_of[10], (FAST, FH, FW), FH ** -0.5, 0.25, ((0, 4),)),
    }


def attend(query_block, key_block, value_block, start_row, window_size, doc_first):
    block_rows = query_block.shape[0]
    key_rows = key_block.shape[0]
    score_scale = query_block.shape[1] ** (-0.5)
    scores = jnp.dot(query_block.astype(jnp.float32), key_block.astype(jnp.float32).T) * score_scale
    query_pos = start_row + jnp.arange(block_rows, dtype=jnp.int32)
    key_pos = start_row - (key_rows - block_rows) + jnp.arange(key_rows, dtype=jnp.int32)
    valid = (key_pos[None, :] <= query_pos[:, None]) & (key_pos[None, :] > query_pos[:, None] - window_size) & (key_pos[None, :] >= doc_first[:, None])
    scores = jnp.where(valid, scores, -1e+30)
    row_max = lax.optimization_barrier(jnp.max(scores, axis=1, keepdims=True))
    weights = jnp.where(valid, jnp.exp(scores - row_max), 0.0)
    weights_bf = (weights / lax.optimization_barrier(jnp.sum(weights, axis=1, keepdims=True))).astype(jnp.bfloat16)
    return jnp.dot(weights_bf, value_block, preferred_element_type=jnp.float32)

def normed(x):
    as_float = x.astype(jnp.float32)
    return (as_float * lax.rsqrt(lax.optimization_barrier(jnp.mean(as_float * as_float, axis=-1, keepdims=True)) + 1e-06)).astype(jnp.bfloat16)

def refresh(old, grad, factor):
    moved = old.astype(jnp.float32) - factor * grad
    kept_norm = jnp.sqrt(lax.optimization_barrier(jnp.sum(old.astype(jnp.float32) ** 2, axis=0, keepdims=True)))
    new_norm = jnp.sqrt(lax.optimization_barrier(jnp.sum(moved * moved, axis=0, keepdims=True)) + 1e-06)
    return (moved * (kept_norm / new_norm)).astype(jnp.bfloat16)

def one_fast(packed):
    q_fast, k_fast, v_fast, rate_fast, rate_head, gate_w, up_w, down_w = packed
    k_norm = normed(k_fast)
    q_norm = normed(q_fast)
    pre_gate = jnp.dot(k_norm, gate_w, preferred_element_type=jnp.float32)
    pre_up = jnp.dot(k_norm, up_w, preferred_element_type=jnp.float32)
    sigmoid_gate = jax.nn.sigmoid(pre_gate)
    lifted = pre_gate * sigmoid_gate
    hidden = (lifted * pre_up).astype(jnp.bfloat16)
    target = (rate_fast.astype(jnp.float32)[:, None] * v_fast.astype(jnp.float32)).astype(jnp.bfloat16)
    back_hidden = -jnp.dot(target, down_w.T, preferred_element_type=jnp.float32)
    grad_down = -jnp.dot(hidden.T, target, preferred_element_type=jnp.float32)
    back_gate = (back_hidden * pre_up * sigmoid_gate * (1.0 + pre_gate * (1.0 - sigmoid_gate))).astype(jnp.bfloat16)
    back_up = (back_hidden * lifted).astype(jnp.bfloat16)
    grad_gate = jnp.dot(k_norm.T, back_gate, preferred_element_type=jnp.float32)
    grad_up = jnp.dot(k_norm.T, back_up, preferred_element_type=jnp.float32)
    new_gate = refresh(gate_w, grad_gate, rate_head * lax.rsqrt(jnp.mean(grad_gate * grad_gate) + 1e-06))
    new_up = refresh(up_w, grad_up, rate_head * lax.rsqrt(jnp.mean(grad_up * grad_up) + 1e-06))
    new_down = refresh(down_w, grad_down, rate_head * lax.rsqrt(jnp.mean(grad_down * grad_down) + 1e-06))
    gate_q = jnp.dot(q_norm, new_gate, preferred_element_type=jnp.float32)
    up_q = jnp.dot(q_norm, new_up, preferred_element_type=jnp.float32)
    applied = (jax.nn.silu(gate_q) * up_q).astype(jnp.bfloat16)
    return jnp.dot(applied, new_down, preferred_element_type=jnp.float32)

def reference(queries, keys, values, step_rate, doc_start, window_len, head_order, learn_rate, w_gate, w_up, w_down):
    block_rows = min(512, TOK_DEV * N_HEAD)
    block_count = TOKENS // block_rows
    query_heads = queries.reshape(TOKENS, HEADS, HD).transpose(1, 0, 2)
    key_heads = jnp.pad(keys.reshape(TOKENS, HEADS, HD).transpose(1, 0, 2), ((0, 0), (WINDOW, 0), (0, 0)))
    value_heads = jnp.pad(values.reshape(TOKENS, HEADS, HD).transpose(1, 0, 2), ((0, 0), (WINDOW, 0), (0, 0)))

    def one_head(packed):
        query_one, key_one, value_one, window_size = packed

        def one_block(block_index):
            start_row = block_index * block_rows
            return attend(lax.dynamic_slice_in_dim(query_one, start_row, block_rows, 0), lax.dynamic_slice_in_dim(key_one, start_row, WINDOW + block_rows, 0), lax.dynamic_slice_in_dim(value_one, start_row, WINDOW + block_rows, 0), start_row, window_size, lax.dynamic_slice_in_dim(doc_start, start_row, block_rows, 0))
        return lax.map(one_block, jnp.arange(block_count, dtype=jnp.int32)).reshape(TOKENS, HD)
    attended = lax.map(one_head, (query_heads, key_heads, value_heads, window_len)).transpose(1, 0, 2)

    def grouped(x):
        return x.reshape(TOKENS, HEADS, HD)[:, head_order].reshape(TOKENS, FAST, FW).transpose(1, 0, 2)
    produced = lax.map(one_fast, (grouped(queries), grouped(keys), grouped(values), step_rate.T, learn_rate, w_gate, w_up, w_down))
    produced = produced.transpose(1, 0, 2).reshape(TOKENS, HEADS, HD)
    placed = jnp.zeros((TOKENS, HEADS, HD), jnp.float32).at[:, head_order].set(produced)
    return (attended + placed).astype(jnp.bfloat16).reshape(TOKENS, D)
```

```python
import functools

import jax
import jax.numpy as jnp
from jax import lax
from jax.experimental import pallas as pl
from jax.experimental.pallas import tpu as pltpu
from jax.sharding import PartitionSpec as P

MESH = pl.DeviceIdType.MESH
ANY = pl.BlockSpec(memory_space=pl.ANY)
VM = pl.BlockSpec(memory_space=pltpu.VMEM)
HD = 128
GH = 5
FW = 640
TB = 128
KVR = 272
ROWS = 8
F32 = jnp.float32
BF16 = jnp.bfloat16

SEND_ORDER = ((0, 1), (1, 0), (3, 0), (1, 1), (3, 1), (2, 0), (2, 1))
WAIT_ORDER = ((0, 0), (0, 1), (1, 0), (3, 0), (1, 1), (3, 1), (2, 0), (2, 1))


def coords():
    s, h = lax.axis_index("seq"), lax.axis_index("head")
    return lax.div(s, 4), lax.rem(s, 4), lax.div(h, 2), lax.rem(h, 2)


def dev(row, z, x, c):
    return (row * 4 + z, x * 2 + c)


def sem_wait_bytes(ref, sem):
    pltpu.make_async_copy(ref, ref, sem).wait()


def signal(sem, device):
    pl.semaphore_signal(sem, inc=1, device_id=device, device_id_type=MESH)


def rcopy(src, dst, ssem, rsem, device):
    return pltpu.make_async_remote_copy(
        src_ref=src, dst_ref=dst, send_sem=ssem, recv_sem=rsem, device_id=device, device_id_type=MESH
    )


def reorder_kernel(order, q, k, v, rate, kvr, qo):
    g = pl.program_id(0)
    for j in range(GH):
        at = pl.ds(pl.multiple_of(order[g * GH + j] * HD, HD), HD)
        to = slice(j * HD, (j + 1) * HD)
        kvr[0, 0:TB, to] = k[:, at]
        kvr[0, TB : 2 * TB, to] = v[:, at]
        qo[0, :, to] = q[:, at]
    kvr[0, 2 * TB :, 0:HD] = rate[0]
    kvr[0, 2 * TB :, HD:] = jnp.zeros((KVR - 2 * TB, FW - HD), BF16)


def reorder(head_order, q, k, v, rate):
    whole = pl.BlockSpec((TB, 40 * HD), lambda g, o: (0, 0))
    return pl.pallas_call(
        reorder_kernel,
        grid_spec=pltpu.PrefetchScalarGridSpec(
            num_scalar_prefetch=1,
            grid=(8,),
            in_specs=[whole, whole, whole, pl.BlockSpec((1, 16, HD), lambda g, o: (g, 0, 0))],
            out_specs=[
                pl.BlockSpec((1, KVR, FW), lambda g, o: (g, 0, 0)),
                pl.BlockSpec((1, TB, FW), lambda g, o: (g, 0, 0)),
            ],
        ),
        out_shape=[
            jax.ShapeDtypeStruct((8, KVR, FW), BF16),
            jax.ShapeDtypeStruct((8, TB, FW), BF16),
        ],
        name="reorder",
    )(head_order, q, k, v, rate)


def scatter_kernel(kvr, q, wg, wu, wd, w2, w1, w0, qb, wrec, lkv, lq, lsem, s_kv, s_q, s_f, s_g, s_r, s_w, r_kv, r_q, r_w0, r_w1, r_w):
    row, z, x, c = coords()
    half = lax.div(z, 2)
    block = lax.rem(z, 2) * 4 + x * 2 + c
    own = half == c
    mine = 4 * x + z
    barrier = pltpu.get_barrier_semaphore()
    for zs in (0, 1):
        for xs in (0, 1):
            for cs in (0, 1):
                zz = 2 * c + zs

                @pl.when(jnp.logical_not((zz == z) & (xs == x) & (cs == c)))
                def _():
                    signal(barrier, dev(row, zz, xs, cs))

    @pl.when((c == 0) & (row > 0))
    def _():
        signal(barrier, dev(row - 1, z, x, 0))
        signal(barrier, dev(row - 1, z, x, 1))

    @pl.when(c == 1)
    def _():
        signal(barrier, dev(row, z, x, 0))

    @pl.when(jnp.logical_not(own))
    def _():
        signal(barrier, dev(row, z, x, 1 - c))

    one = lambda p: p.astype(jnp.int32)
    pl.semaphore_wait(barrier, 8 - one(own) + one(row < ROWS - 1) + one(c == 0) + one(own))

    @pl.when(own)
    def _():
        pltpu.make_async_copy(kvr.at[mine], lkv, lsem.at[0]).start()
        pltpu.make_async_copy(q.at[mine], lq, lsem.at[1]).start()

    @pl.when(jnp.logical_not(own))
    def _():
        rcopy(kvr.at[mine], w2.at[block], s_kv.at[7], r_kv.at[block], dev(row, z, x, 1 - c)).start()

    def target(dz, dx):
        zt, xt = lax.rem(z + dz, 4), lax.rem(x + dx, 2)
        return 4 * xt + zt, dev(row, zt, xt, half)

    for n, (dz, dx) in enumerate(SEND_ORDER):
        g, to = target(dz, dx)
        rcopy(kvr.at[g], w2.at[block], s_kv.at[n], r_kv.at[block], to).start()

    @pl.when(own)
    def _():
        for n, w in enumerate((wg, wu, wd)):
            rcopy(w.at[lax.rem(z, 2)], wrec.at[n], s_w.at[n], r_w.at[n], dev(row, z, x, 1 - c)).start()

    for n, (dz, dx) in enumerate(SEND_ORDER):
        g, to = target(dz, dx)
        rcopy(q.at[g], qb.at[block], s_q.at[n], r_q.at[block], to).start()

    @pl.when(jnp.logical_not(own))
    def _():
        rcopy(q.at[mine], qb.at[block], s_q.at[7], r_q.at[block], dev(row, z, x, 1 - c)).start()

    @pl.when(own)
    def _():
        sem_wait_bytes(lkv, lsem.at[0])
        pltpu.make_async_copy(lkv, w2.at[block], r_kv.at[block]).start()
        sem_wait_bytes(lq, lsem.at[1])
        pltpu.make_async_copy(lq, qb.at[block], r_q.at[block]).start()

    for dz, dx in WAIT_ORDER:
        zs, xs = lax.rem(z + 4 - dz, 4), lax.rem(x + dx, 2)

        @pl.when(lax.div(zs, 2) == c)
        def _():
            for cs in (0, 1):
                b = lax.rem(zs, 2) * 4 + xs * 2 + cs
                sem_wait_bytes(w2.at[b], r_kv.at[b])
                kv = w2.at[b, pl.ds(0, 2 * TB)]

                @pl.when((row < ROWS - 1) & (c == 0))
                def _():
                    rcopy(kv, w0.at[b], s_f.at[b], r_w0.at[b], dev(row + 1, z, x, 0)).start()

                @pl.when((row < ROWS - 1) & (c == 1))
                def _():
                    rcopy(kv, w1.at[b], s_f.at[b], r_w1.at[b], dev(row + 1, z, x, 0)).start()

                @pl.when(c == 0)
                def _():
                    rcopy(kv, w1.at[b], s_g.at[b], r_w1.at[b], dev(row, z, x, 1)).start()

    @pl.when((c == 0) & (row > 0))
    def _():
        for dz, dx in WAIT_ORDER:
            zs, xs = lax.rem(z + 4 - dz, 4), lax.rem(x + dx, 2)

            @pl.when(lax.div(zs, 2) == 1)
            def _():
                for cs in (0, 1):
                    b = lax.rem(zs, 2) * 4 + xs * 2 + cs
                    sem_wait_bytes(w1.at[b], r_w1.at[b])
                    rcopy(w1.at[b], w0.at[b], s_r.at[b], r_w0.at[b], dev(row, z, x, 1)).start()

        for b in range(8):
            sem_wait_bytes(w1.at[b], s_r.at[b])

    @pl.when(row > 0)
    def _():
        for b in range(8):
            sem_wait_bytes(w0.at[b], r_w0.at[b])

    @pl.when(c == 1)
    def _():
        for b in range(8):
            sem_wait_bytes(w1.at[b], r_w1.at[b])

    @pl.when(c == 0)
    def _():
        for b in range(8):
            sem_wait_bytes(w1.at[b], s_g.at[b])

    @pl.when(row < ROWS - 1)
    def _():
        for b in range(8):
            sem_wait_bytes(w1.at[b], s_f.at[b])

    for b in range(8):
        sem_wait_bytes(qb.at[b], r_q.at[b])
    for n in range(7):
        sem_wait_bytes(w2.at[n], s_kv.at[n])
        sem_wait_bytes(qb.at[n], s_q.at[n])

    @pl.when(jnp.logical_not(own))
    def _():
        sem_wait_bytes(w2.at[7], s_kv.at[7])
        sem_wait_bytes(qb.at[7], s_q.at[7])
        for n in range(3):
            sem_wait_bytes(wrec.at[n], r_w.at[n])

    @pl.when(own)
    def _():
        for n in range(3):
            sem_wait_bytes(wrec.at[n], s_w.at[n])


def scatter(kvr, q, wg, wu, wd):
    dma = pltpu.SemaphoreType.DMA
    return pl.pallas_call(
        scatter_kernel,
        in_specs=[ANY] * 5,
        out_specs=[ANY] * 5,
        out_shape=[
            jax.ShapeDtypeStruct((8, KVR, FW), BF16),
            jax.ShapeDtypeStruct((8, 2 * TB, FW), BF16),
            jax.ShapeDtypeStruct((8, 2 * TB, FW), BF16),
            jax.ShapeDtypeStruct((8, TB, FW), BF16),
            jax.ShapeDtypeStruct((3, FW, FW), BF16),
        ],
        scratch_shapes=[
            pltpu.VMEM((KVR, FW), BF16),
            pltpu.VMEM((TB, FW), BF16),
            dma((2,)),
        ]
        + [dma((8,))] * 5
        + [dma((3,))]
        + [dma((8,))] * 4
        + [dma((3,))],
        compiler_params=pltpu.CompilerParams(collective_id=0, has_side_effects=True),
        name="scatter",
    )(kvr, q, wg, wu, wd)


def fetch_weights(ws, wrec, wbuf, sem):
    _, z, x, c = coords()

    @pl.when(lax.div(z, 2) == c)
    def _():
        for n in range(3):
            pltpu.make_async_copy(ws[n].at[lax.rem(z, 2)], wbuf.at[n], sem.at[n]).start()

    @pl.when(lax.div(z, 2) != c)
    def _():
        for n in range(3):
            pltpu.make_async_copy(wrec.at[n], wbuf.at[n], sem.at[n]).start()


def dot(a, b, dims):
    return lax.dot_general(a, b, (dims, ((), ())), preferred_element_type=F32)


def normed(x):
    x = x.astype(F32)
    return (x * lax.rsqrt(jnp.mean(x * x, axis=-1, keepdims=True) + 1e-6)).astype(BF16)


def grads_kernel(wg, wu, wd, wrec, w2, grad, wbuf, kn, hid, tgt, bgu, sem):
    fetch_weights((wg, wu, wd), wrec, wbuf, sem)
    for n in range(3):
        sem_wait_bytes(wbuf.at[n], sem.at[n])

    def tile(b, _):
        rows = pl.ds(pl.multiple_of(b * TB, TB), TB)
        k = normed(w2[b, 0:TB, :])
        kn[rows, :] = k
        rate = w2[b, 2 * TB : KVR, 0:HD].astype(F32)[0:1]
        rate = jnp.broadcast_to(rate, (TB, TB)).T
        for j in range(GH):
            at = slice(j * HD, (j + 1) * HD)
            tgt[rows, at] = (rate * w2[b, TB : 2 * TB, at].astype(F32)).astype(BF16)
        pre_gate = dot(k, wbuf[0], ((1,), (0,)))
        pre_up = dot(k, wbuf[1], ((1,), (0,)))
        back = -dot(tgt[rows, :], wbuf[2], ((1,), (1,)))
        sig = jax.nn.sigmoid(pre_gate)
        lifted = pre_gate * sig
        hid[rows, :] = (lifted * pre_up).astype(BF16)
        bgu[rows, 0:FW] = (back * pre_up * sig * (1.0 + pre_gate * (1.0 - sig))).astype(BF16)
        bgu[rows, FW:] = (back * lifted).astype(BF16)
        return 0

    lax.fori_loop(0, 8, tile, 0)

    def out(i, _):
        at = pl.ds(pl.multiple_of(i * HD, HD), HD)
        both = dot(kn[:, at], bgu[...], ((0,), (0,)))
        grad[0, at, :] = both[:, 0:FW].astype(BF16)
        grad[1, at, :] = both[:, FW:].astype(BF16)
        grad[2, at, :] = (-dot(hid[:, at], tgt[...], ((0,), (0,)))).astype(BF16)
        return 0

    lax.fori_loop(0, GH, out, 0)


def grads(wg, wu, wd, wrec, w2):
    return pl.pallas_call(
        grads_kernel,
        in_specs=[ANY] * 4 + [VM],
        out_specs=VM,
        out_shape=jax.ShapeDtypeStruct((3, FW, FW), BF16),
        scratch_shapes=[
            pltpu.VMEM((3, FW, FW), BF16),
            pltpu.VMEM((8 * TB, FW), BF16),
            pltpu.VMEM((8 * TB, FW), BF16),
            pltpu.VMEM((8 * TB, FW), BF16),
            pltpu.VMEM((8 * TB, 2 * FW), BF16),
            pltpu.SemaphoreType.DMA((3,)),
        ],
        name="grads",
    )(wg, wu, wd, wrec, w2)


HALF = FW // 2
PART = FW // 8


def reduce_kernel(grad, out, r0, h, r1, part, r2, s0, t0, s1, t1, s2, t2, s3, t3, s4, t4):
    row, z, x, c = coords()
    y, xh = lax.rem(row, 4), lax.div(row, 4)
    partner = dev(row, z, x, 1 - c)
    across = dev((1 - xh) * 4 + y, z, x, c)
    peer = lambda k: lax.rem(y + k, 4)
    peer_dev = lambda k: dev(xh * 4 + peer(k), z, x, c)
    barrier = pltpu.get_barrier_semaphore()
    signal(barrier, partner)
    signal(barrier, across)
    for k in (1, 2, 3):
        signal(barrier, peer_dev(k))
    pl.semaphore_wait(barrier, 5)
    order = (2, 1, 3, 0)
    rows = lambda core, k: pl.ds(pl.multiple_of(core * HALF + peer(k) * PART, 16), PART)
    for k in order:
        rcopy(grad.at[:, rows(1 - c, k), :], r0.at[peer(k)], s0.at[k], t0.at[peer(k)], partner).start()
    for k in order:
        j = peer(k)
        sem_wait_bytes(r0.at[j], t0.at[j])
        total = grad[:, rows(c, k), :].astype(F32) + r0[j].astype(F32)
        if k:
            h[k] = total.astype(BF16)
            rcopy(h.at[k], r1.at[4 - k], s1.at[k], t1.at[4 - k], peer_dev(k)).start()
    for k in (1, 3, 2):
        sem_wait_bytes(r1.at[k], t1.at[k])
        total = total + r1[k].astype(F32)
    part[0] = total.astype(BF16)
    rcopy(part.at[0], r2, s2, t2, across).start()
    sem_wait_bytes(r2, t2)
    mine = rows(c, 0)
    out[:, mine, :] = (part[0].astype(F32) + r2[...].astype(F32)).astype(BF16)
    for k in (2, 1, 3):
        rcopy(out.at[:, mine, :], out.at[:, mine, :], s3.at[k], t3.at[4 - k], peer_dev(k)).start()
    rcopy(out.at[:, mine, :], out.at[:, mine, :], s4.at[0], t4.at[y], partner).start()
    for k in (1, 3, 2):
        got = out.at[:, rows(c, k), :]
        sem_wait_bytes(r2, t3.at[k])
        rcopy(got, got, s4.at[k], t4.at[peer(k)], partner).start()
    for k in range(4):
        sem_wait_bytes(r2, t4.at[k])
        sem_wait_bytes(r2, s0.at[k])
        sem_wait_bytes(r2, s4.at[k])
        if k:
            sem_wait_bytes(r2, s1.at[k])
            sem_wait_bytes(r2, s3.at[k])
    sem_wait_bytes(r2, s2)


def reduce_grads(grad):
    dma = pltpu.SemaphoreType.DMA
    piece = (3, PART, FW)
    return pl.pallas_call(
        reduce_kernel,
        in_specs=[VM],
        out_specs=VM,
        out_shape=jax.ShapeDtypeStruct((3, FW, FW), BF16),
        scratch_shapes=[
            pltpu.VMEM((4,) + piece, BF16),
            pltpu.VMEM((4,) + piece, BF16),
            pltpu.VMEM((4,) + piece, BF16),
            pltpu.VMEM((1,) + piece, BF16),
            pltpu.VMEM(piece, BF16),
            dma((4,)),
            dma((4,)),
            dma((4,)),
            dma((4,)),
            dma,
            dma,
            dma((4,)),
            dma((4,)),
            dma((4,)),
            dma((4,)),
        ],
        compiler_params=pltpu.CompilerParams(collective_id=1, has_side_effects=True),
        name="reduce",
    )(grad)


TQ = 256
TK = 256
SCALE = HD**-0.5 * 1.4426950408889634


def attend_kernel(order, window, first, q, w0, w1, w2, doc, o, k_all, v_all):
    row, z, x, c = coords()
    head = order[(4 * x + z) * GH + pl.program_id(0)]
    win = window[head]
    start = row * 2048 + c * 1024
    for n, w in enumerate((w0, w1, w2)):
        for b in range(8):
            at = slice(n * 1024 + b * TB, n * 1024 + (b + 1) * TB)
            k_all[at, :] = w[b, 0:TB, :]
            v_all[at, :] = w[b, TB : 2 * TB, :]

    for i in range(1024 // TQ):
        qt = q[2 * i : 2 * i + 2].reshape(TQ, HD)
        pos0 = start + i * TQ
        row_low = jnp.maximum(doc[i * TQ : (i + 1) * TQ, :], pos0 + lax.broadcasted_iota(jnp.int32, (TQ, HD), 0) - win + 1)
        low_first = jnp.maximum(first[i * TQ], pos0 - win + 1)
        low_last = jnp.maximum(first[i * TQ + TQ - 1], pos0 + TQ - win)
        base = start - 2048
        lo = lax.div(low_first - base, TK)
        hi = (2048 + i * TQ) // TK

        def chunk(j, carry, masked):
            m, l, acc = carry
            at = pl.ds(pl.multiple_of(j * TK, TK), TK)
            s = dot(qt, k_all[at, :], ((1,), (1,)))
            if masked:
                kp = base + j * TK + lax.broadcasted_iota(jnp.int32, (TQ, TK), 1)
                qp = pos0 + lax.broadcasted_iota(jnp.int32, (TQ, TK), 0)
                low = jnp.concatenate([row_low] * (TK // HD), axis=1)
                s = jnp.where((kp <= qp) & (kp >= low), s, -1e30)
            m_new = jnp.maximum(m, jnp.max(s, axis=1, keepdims=True))
            p = jnp.exp2((s - m_new) * SCALE)
            if masked:
                p = jnp.where(s > -1e29, p, 0.0)
            a = jnp.exp2((m - m_new) * SCALE)
            l = a * l + jnp.sum(p, axis=1, keepdims=True)
            acc = a * acc + dot(p.astype(BF16), v_all[at, :], ((1,), (0,)))
            return m_new, l, acc

        def step(j, carry):
            whole = base + j * TK >= low_last
            return lax.cond(whole, lambda cr: chunk(j, cr, False), lambda cr: chunk(j, cr, True), carry)

        zero = (jnp.full((TQ, 1), -1e30, F32), jnp.zeros((TQ, 1), F32), jnp.zeros((TQ, HD), F32))
        carry = chunk(hi, zero, True)
        m, l, acc = lax.fori_loop(lo, hi, step, carry)
        o[i * TQ : (i + 1) * TQ, :] = acc / l


def attend(order, window, first, q, w0, w1, w2, doc):
    def lane(rows, depth):
        return pl.BlockSpec((depth, rows, HD), lambda h, *_: (0, 0, h))

    return pl.pallas_call(
        attend_kernel,
        grid_spec=pltpu.PrefetchScalarGridSpec(
            num_scalar_prefetch=3,
            grid=(GH,),
            in_specs=[
                lane(TB, 8),
                lane(2 * TB, 8),
                lane(2 * TB, 8),
                lane(2 * TB, 8),
                pl.BlockSpec((1024, HD), lambda h, *_: (0, 0)),
            ],
            out_specs=pl.BlockSpec((1024, HD), lambda h, *_: (0, h)),
            scratch_shapes=[pltpu.VMEM((3072, HD), BF16), pltpu.VMEM((3072, HD), BF16)],
        ),
        out_shape=jax.ShapeDtypeStruct((1024, FW), F32),
        name="attend",
    )(order, window, first, q, w0, w1, w2, doc)


def apply_kernel(rates, wg, wu, wd, wrec, grad, q, att, o, wbuf, new, sem):
    fetch_weights((wg, wu, wd), wrec, wbuf, sem)
    _, z, x, c = coords()
    rate = rates[4 * x + z]
    for n in range(3):
        sem_wait_bytes(wbuf.at[n], sem.at[n])

        def square(i, s):
            g = grad[n, pl.ds(pl.multiple_of(i * 32, 32), 32), :].astype(F32)
            return s + g * g

        total = lax.fori_loop(0, FW // 32, square, jnp.zeros((32, FW), F32))
        mean = jnp.sum(jnp.sum(total, axis=0, keepdims=True), axis=1, keepdims=True) * (1.0 / (FW * FW))
        factor = rate * lax.rsqrt(mean + 1e-6)

        def column(i, _):
            at = pl.ds(pl.multiple_of(i * HD, HD), HD)
            old = wbuf[n, :, at].astype(F32)
            moved = old - factor * grad[n, :, at].astype(F32)
            kept = jnp.sqrt(jnp.sum(old * old, axis=0, keepdims=True))
            fresh = jnp.sqrt(jnp.sum(moved * moved, axis=0, keepdims=True) + 1e-6)
            new[n, :, at] = (moved * (kept / fresh)).astype(BF16)
            return 0

        lax.fori_loop(0, GH, column, 0)

    def tile(b, _):
        qn = normed(q[b])
        gate = dot(qn, new[0], ((1,), (0,)))
        up = dot(qn, new[1], ((1,), (0,)))
        applied = (gate * jax.nn.sigmoid(gate) * up).astype(BF16)
        out = dot(applied, new[2], ((1,), (0,)))
        rows = pl.ds(pl.multiple_of(b * TB, TB), TB)
        o[b] = (out + att[rows, :]).astype(BF16)
        return 0

    lax.fori_loop(0, 8, tile, 0)


def apply(rates, wg, wu, wd, wrec, grad, q, att):
    return pl.pallas_call(
        apply_kernel,
        in_specs=[pl.BlockSpec(memory_space=pltpu.SMEM)] + [ANY] * 4 + [VM] * 3,
        out_specs=VM,
        out_shape=jax.ShapeDtypeStruct((8, TB, FW), BF16),
        scratch_shapes=[
            pltpu.VMEM((3, FW, FW), BF16),
            pltpu.VMEM((3, FW, FW), BF16),
            pltpu.SemaphoreType.DMA((3,)),
        ],
        name="apply",
    )(rates, wg, wu, wd, wrec, grad, q, att)


def gather_kernel(a, out, buf, lsem, ssem, rsem):
    row, z, x, c = coords()
    half = lax.div(z, 2)
    own = half == c
    mine = 4 * x + z
    block = lax.rem(z, 2) * 4 + x * 2 + c
    barrier = pltpu.get_barrier_semaphore()

    for dz in range(4):
        for dx in range(2):
            zs, xs = lax.rem(z + dz, 4), lax.rem(x + dx, 2)
            if (dz, dx) == (0, 0):

                @pl.when(jnp.logical_not(own))
                def _():
                    signal(barrier, dev(row, zs, xs, half))
            else:
                signal(barrier, dev(row, zs, xs, half))
    pl.semaphore_wait(barrier, 8 - own.astype(jnp.int32))

    @pl.when(own)
    def _():
        pltpu.make_async_copy(a.at[block], buf, lsem).start()

    order = ((0, 1), (1, 0), (1, 1), (3, 0), (3, 1), (2, 0), (2, 1), (0, 0))
    for dz, dx in order:
        zt, xt = lax.rem(z + dz, 4), lax.rem(x + dx, 2)

        @pl.when(lax.div(zt, 2) == c)
        def _():
            for ct in (0, 1):
                b = lax.rem(zt, 2) * 4 + xt * 2 + ct
                if (dz, dx) == (0, 0):

                    @pl.when(ct != c)
                    def _():
                        rcopy(a.at[b], out.at[mine], ssem.at[b], rsem.at[mine], dev(row, zt, xt, ct)).start()
                else:
                    rcopy(a.at[b], out.at[mine], ssem.at[b], rsem.at[mine], dev(row, zt, xt, ct)).start()

    @pl.when(own)
    def _():
        sem_wait_bytes(buf, lsem)
        pltpu.make_async_copy(buf, out.at[mine], rsem.at[mine]).start()

    for g in range(8):
        sem_wait_bytes(buf, rsem.at[g])
    for b in range(8):

        @pl.when(jnp.logical_not(own & (block == b)))
        def _():
            sem_wait_bytes(buf, ssem.at[b])


def gather(a):
    dma = pltpu.SemaphoreType.DMA
    return pl.pallas_call(
        gather_kernel,
        in_specs=[ANY],
        out_specs=ANY,
        out_shape=jax.ShapeDtypeStruct((8, TB, FW), BF16),
        scratch_shapes=[pltpu.VMEM((TB, FW), BF16), dma, dma((8,)), dma((8,))],
        compiler_params=pltpu.CompilerParams(collective_id=2, has_side_effects=True),
        name="gather",
    )(a)


def restore_kernel(order, a, o):
    for g in range(8):
        for j in range(GH):
            at = pl.ds(pl.multiple_of(order[g * GH + j] * HD, HD), HD)
            o[:, at] = a[g, :, j * HD : (j + 1) * HD]


def restore(order, a):
    return pl.pallas_call(
        restore_kernel,
        grid_spec=pltpu.PrefetchScalarGridSpec(
            num_scalar_prefetch=1,
            grid=(4,),
            in_specs=[pl.BlockSpec((8, TB // 4, FW), lambda i, o: (0, i, 0))],
            out_specs=pl.BlockSpec((TB // 4, 40 * HD), lambda i, o: (i, 0)),
        ),
        out_shape=jax.ShapeDtypeStruct((TB, 40 * HD), BF16),
        name="restore",
    )(order, a)


def per_device(queries, keys, values, step_rate, doc_start, window_len, head_order, learn_rate, w_gate, w_up, w_down):
    rate = jnp.broadcast_to(step_rate.T[:, None, :], (8, 16, TB))
    kvr, q = reorder(head_order, queries, keys, values, rate)
    w2, w1, w0, qb, wrec = scatter(kvr, q, w_gate, w_up, w_down)
    c = lax.rem(lax.axis_index("head"), 2)
    row = lax.div(lax.axis_index("seq"), 4)
    first = lax.dynamic_slice_in_dim(doc_start, row * 2048 + c * 1024, 1024)
    doc = jnp.broadcast_to(first[:, None], (1024, HD))
    grad = reduce_grads(grads(w_gate, w_up, w_down, wrec, w2))
    att = attend(head_order, window_len, first, qb, w0, w1, w2, doc)
    mixed = apply(learn_rate, w_gate, w_up, w_down, wrec, grad, qb, att)
    return restore(head_order, gather(mixed))


def solution(mesh):
    both = P(("seq", "head"), None)
    placed = (both, both, both, both, P(), P(), P(), P()) + (P("head", None, None),) * 3
    return jax.shard_map(per_device, mesh=mesh, in_specs=placed, out_specs=both, check_vma=False)
```

```python
import functools

import jax
import jax.numpy as jnp
from jax import lax
from jax.experimental import pallas as pl
from jax.experimental.pallas import tpu as pltpu
from jax.sharding import PartitionSpec as P

MESH = pl.DeviceIdType.MESH
ANY = pl.BlockSpec(memory_space=pl.ANY)
VM = pl.BlockSpec(memory_space=pltpu.VMEM)
HD = 128
GH = 5
FW = 640
TB = 128
KVR = 272
ROWS = 8
F32 = jnp.float32
BF16 = jnp.bfloat16

SEND_ORDER = ((0, 1), (1, 0), (3, 0), (1, 1), (3, 1), (2, 0), (2, 1))


def coords():
    s, h = lax.axis_index("seq"), lax.axis_index("head")
    return lax.div(s, 4), lax.rem(s, 4), lax.div(h, 2), lax.rem(h, 2)


def dev(row, z, x, c):
    return (row * 4 + z, x * 2 + c)


def sem_wait_bytes(ref, sem):
    pltpu.make_async_copy(ref, ref, sem).wait()


def signal(sem, device):
    pl.semaphore_signal(sem, inc=1, device_id=device, device_id_type=MESH)


def rcopy(src, dst, ssem, rsem, device):
    return pltpu.make_async_remote_copy(
        src_ref=src, dst_ref=dst, send_sem=ssem, recv_sem=rsem, device_id=device, device_id_type=MESH
    )


def reorder_kernel(order, q, k, v, rate, kvr, qo):
    g = pl.program_id(0)
    for j in range(GH):
        at = pl.ds(pl.multiple_of(order[g * GH + j] * HD, HD), HD)
        to = slice(j * HD, (j + 1) * HD)
        kvr[0, 0:TB, to] = k[:, at]
        kvr[0, TB : 2 * TB, to] = v[:, at]
        qo[0, :, to] = q[:, at]
    kvr[0, 2 * TB :, 0:HD] = rate[0]
    kvr[0, 2 * TB :, HD:] = jnp.zeros((KVR - 2 * TB, FW - HD), BF16)


def reorder(head_order, q, k, v, rate):
    whole = pl.BlockSpec((TB, 40 * HD), lambda g, o: (0, 0))
    return pl.pallas_call(
        reorder_kernel,
        grid_spec=pltpu.PrefetchScalarGridSpec(
            num_scalar_prefetch=1,
            grid=(8,),
            in_specs=[whole, whole, whole, pl.BlockSpec((1, 16, HD), lambda g, o: (g, 0, 0))],
            out_specs=[
                pl.BlockSpec((1, KVR, FW), lambda g, o: (g, 0, 0)),
                pl.BlockSpec((1, TB, FW), lambda g, o: (g, 0, 0)),
            ],
        ),
        out_shape=[
            jax.ShapeDtypeStruct((8, KVR, FW), BF16),
            jax.ShapeDtypeStruct((8, TB, FW), BF16),
        ],
        name="reorder",
    )(head_order, q, k, v, rate)

SCALE = HD**-0.5 * 1.4426950408889634
TQ = 256
TK = 512
HALF = FW // 2
PART = FW // 8
LOW = -1e30


def dot(a, b, dims):
    return lax.dot_general(a, b, (dims, ((), ())), preferred_element_type=F32)


def normed(x):
    x = x.astype(F32)
    return (x * lax.rsqrt(jnp.mean(x * x, axis=-1, keepdims=True) + 1e-6)).astype(BF16)


def column(row):
    return jnp.broadcast_to(row, (TB, TB)).T


def layer_kernel(
    kvr, q, wg, wu, wd, rates, wins, out,
    w2, w1, w0, qb, wb, kn, hid, tgt, bgu, grad, r0, h, r1, tot, part, r2, gsum, new, docs, kh, vh, ms, ls, accs, att, mixed,
    s_l, s_kv, s_q, s_f, s_g, s_r, s_w, r_kv, r_q, r_w0, r_w1, r_w, s0, t0, s1, t1, s2, t2, s3, t3, s4, t4, s_o, r_o,
):
    row, z, x, c = coords()
    half = lax.div(z, 2)
    block = lax.rem(z, 2) * 4 + x * 2 + c
    own = half == c
    mine = 4 * x + z
    y, xh = lax.rem(row, 4), lax.div(row, 4)
    partner = dev(row, z, x, 1 - c)
    across = dev((1 - xh) * 4 + y, z, x, c)
    peer = lambda k: lax.rem(y + k, 4)
    peer_dev = lambda k: dev(xh * 4 + peer(k), z, x, c)
    last = row == ROWS - 1
    one = lambda p: p.astype(jnp.int32)

    barrier = pltpu.get_barrier_semaphore()
    for dz in range(4):
        for dx in range(2):
            for dc in range(2):
                if dz or dx or dc:
                    signal(barrier, dev(row, lax.rem(z + dz, 4), lax.rem(x + dx, 2), lax.rem(c + dc, 2)))
    for k in (1, 2, 3):
        signal(barrier, peer_dev(k))
    signal(barrier, across)

    @pl.when((c == 0) & (row > 0))
    def _():
        signal(barrier, dev(row - 1, z, x, 0))
        signal(barrier, dev(row - 1, z, x, 1))

    @pl.when(own)
    def _():
        pltpu.make_async_copy(kvr.at[mine], w2.at[block], r_kv.at[block]).start()
        pltpu.make_async_copy(q.at[mine], qb.at[block], r_q.at[block]).start()
        for n, w in enumerate((wg, wu, wd)):
            pltpu.make_async_copy(w.at[lax.rem(z, 2)], wb.at[n], r_w.at[n]).start()

    @pl.when(row == 0)
    def _():
        w0[...] = jnp.zeros_like(w0)

    @pl.when((row == 0) & (c == 0))
    def _():
        w1[...] = jnp.zeros_like(w1)

    pl.semaphore_wait(barrier, 19 + one(jnp.logical_not(last)))

    def target(dz, dx):
        zt, xt = lax.rem(z + dz, 4), lax.rem(x + dx, 2)
        return 4 * xt + zt, dev(row, zt, xt, half)

    @pl.when(jnp.logical_not(own))
    def _():
        rcopy(kvr.at[mine], w2.at[block], s_kv.at[7], r_kv.at[block], partner).start()

    for n, (dz, dx) in enumerate(SEND_ORDER):
        g, to = target(dz, dx)
        rcopy(kvr.at[g], w2.at[block], s_kv.at[n], r_kv.at[block], to).start()

    @pl.when(own)
    def _():
        for n, w in enumerate((wg, wu, wd)):
            rcopy(w.at[lax.rem(z, 2)], wb.at[n], s_w.at[n], r_w.at[n], partner).start()

    for n, (dz, dx) in enumerate(SEND_ORDER):
        g, to = target(dz, dx)
        rcopy(q.at[g], qb.at[block], s_q.at[n], r_q.at[block], to).start()

    @pl.when(jnp.logical_not(own))
    def _():
        rcopy(q.at[mine], qb.at[block], s_q.at[7], r_q.at[block], partner).start()

    for n in range(3):
        sem_wait_bytes(wb.at[n], r_w.at[n])

    near = jnp.where(own, lax.rem(z, 2), jnp.where(z == 0, 1, jnp.where(z == 3, 0, 1 - lax.rem(z, 2))))

    def nth(n, z_first):
        zs = lax.rem(z_first + lax.div(n, 4), 2)
        xs = lax.rem(x + lax.rem(lax.div(n, 2), 2), 2)
        return zs * 4 + xs * 2 + lax.rem(n, 2)

    def arrive(n, _):
        b = nth(n, near)
        sem_wait_bytes(w2.at[b], r_kv.at[b])
        kv = w2.at[b, pl.ds(0, 2 * TB)]

        @pl.when(jnp.logical_not(last) & (c == 0))
        def _():
            rcopy(kv, w0.at[b], s_f.at[b], r_w0.at[b], dev(row + 1, z, x, 0)).start()

        @pl.when(jnp.logical_not(last) & (c == 1))
        def _():
            rcopy(kv, w1.at[b], s_f.at[b], r_w1.at[b], dev(row + 1, z, x, 0)).start()

        @pl.when(c == 0)
        def _():
            rcopy(kv, w1.at[b], s_g.at[b], r_w1.at[b], partner).start()

        rows = pl.ds(pl.multiple_of(b * TB, TB), TB)
        k = normed(w2[b, 0:TB, :])
        kn[rows, :] = k
        extra = w2[b, 2 * TB : KVR, 0:HD].astype(F32)
        docs[rows, :] = column(extra[1:2]) * float(TB) + column(extra[2:3])
        rate = column(extra[0:1])
        for j in range(GH):
            at = slice(j * HD, (j + 1) * HD)
            tgt[rows, at] = (rate * w2[b, TB : 2 * TB, at].astype(F32)).astype(BF16)
        pre_gate = dot(k, wb[0], ((1,), (0,)))
        pre_up = dot(k, wb[1], ((1,), (0,)))
        back = -dot(tgt[rows, :], wb[2], ((1,), (1,)))
        sig = jax.nn.sigmoid(pre_gate)
        lifted = pre_gate * sig
        hid[rows, :] = (lifted * pre_up).astype(BF16)
        bgu[rows, 0:FW] = (back * pre_up * sig * (1.0 + pre_gate * (1.0 - sig))).astype(BF16)
        bgu[rows, FW:] = (back * lifted).astype(BF16)
        return 0

    lax.fori_loop(0, 8, arrive, 0)

    def grad_rows(i, _):
        at = pl.ds(pl.multiple_of(i * HD, HD), HD)
        both = dot(kn[:, at], bgu[...], ((0,), (0,)))
        grad[0, at, :] = both[:, 0:FW].astype(BF16)
        grad[1, at, :] = both[:, FW:].astype(BF16)
        grad[2, at, :] = (-dot(hid[:, at], tgt[...], ((0,), (0,)))).astype(BF16)
        return 0

    lax.fori_loop(0, GH, grad_rows, 0)

    rows_of = lambda core, k: pl.ds(pl.multiple_of(core * HALF + peer(k) * PART, 16), PART)
    order = (2, 1, 3, 0)
    for k in order:
        rcopy(grad.at[:, rows_of(1 - c, k), :], r0.at[k], s0.at[k], t0.at[k], partner).start()
    for k in order:
        sem_wait_bytes(r0.at[k], t0.at[k])
        total = grad[:, rows_of(c, k), :].astype(F32) + r0[k].astype(F32)
        if k:
            h[k] = total.astype(BF16)
            rcopy(h.at[k], r1.at[4 - k], s1.at[k], t1.at[4 - k], peer_dev(k)).start()
        else:
            tot[...] = total

    def reduce_y():
        for k in (1, 3, 2):
            sem_wait_bytes(r1.at[k], t1.at[k])
        total = tot[...] + r1[1].astype(F32) + r1[2].astype(F32) + r1[3].astype(F32)
        part[...] = total.astype(BF16)
        rcopy(part, r2, s2, t2, across).start()

    def reduce_x():
        sem_wait_bytes(r2, t2)
        at = rows_of(c, 0)
        gsum[:, at, :] = (part[...].astype(F32) + r2[...].astype(F32)).astype(BF16)
        done = gsum.at[:, at, :]
        for k in (2, 1, 3):
            rcopy(done, done, s3.at[k], t3.at[4 - k], peer_dev(k)).start()
        rcopy(done, done, s4.at[0], t4.at[y], partner).start()

    def reduce_end():
        for k in (1, 3, 2):
            got = gsum.at[:, rows_of(c, k), :]
            sem_wait_bytes(r2, t3.at[k])
            rcopy(got, got, s4.at[k], t4.at[peer(k)], partner).start()
        for k in range(4):
            sem_wait_bytes(r2, t4.at[k])

    @pl.when((c == 0) & (row > 0))
    def _():
        def relay(n, _):
            b = nth(n, jnp.where(half == 1, lax.rem(z, 2), 1 - z))
            sem_wait_bytes(w1.at[b], r_w1.at[b])
            rcopy(w1.at[b], w0.at[b], s_r.at[b], r_w0.at[b], partner).start()
            return 0

        lax.fori_loop(0, 8, relay, 0)

    @pl.when(row > 0)
    def _():
        for b in range(8):
            sem_wait_bytes(w0.at[b], r_w0.at[b])

    @pl.when(c == 1)
    def _():
        for b in range(8):
            sem_wait_bytes(w1.at[b], r_w1.at[b])

    for b in range(8):
        sem_wait_bytes(qb.at[b], r_q.at[b])

    base = (row * 2048 + c * 1024 - 2048).astype(F32)
    lane = lax.broadcasted_iota(jnp.int32, (TQ, HD), 1).astype(F32)
    down = lax.broadcasted_iota(jnp.int32, (TQ, HD), 0).astype(F32)

    def head(hh, _):
        at = pl.ds(pl.multiple_of(hh * HD, HD), HD)
        win = wins[mine * GH + hh].astype(F32)
        for n, w in enumerate((w0, w1, w2)):
            for b in range(8):
                rows = slice(n * 1024 + b * TB, n * 1024 + (b + 1) * TB)
                kh[rows, :] = w[b, 0:TB, at]
                vh[rows, :] = w[b, TB : 2 * TB, at]

        def chunk(i, first, width, start):
            keys = pl.ds(first if isinstance(first, int) else pl.multiple_of(first, TQ), width)
            qt = qb[2 * i : 2 * i + 2, :, at].reshape(TQ, HD)
            s = dot(qt, kh[keys, :], ((1,), (1,)))
            off = first.astype(F32) if not isinstance(first, int) else float(first)
            low = jnp.maximum(docs[i * TQ : (i + 1) * TQ, :] - base, down + (2049.0 + TQ * i) - win) - off
            parts = []
            for t in range(width // HD):
                seen = lane >= low - float(HD * t)
                if start:
                    seen = seen & (lane <= down + float(width - TQ - HD * t))
                parts.append(jnp.where(seen, s[:, t * HD : (t + 1) * HD], LOW))
            top = functools.reduce(jnp.maximum, parts)
            top = jnp.broadcast_to(jnp.max(top, axis=1, keepdims=True), (TQ, HD))
            if not start:
                before = ms[i]
                top = jnp.maximum(before, top)
            ms[i] = top
            ps = [jnp.exp2((p - top) * SCALE) for p in parts]
            total = functools.reduce(jnp.add, ps)
            got = dot(jnp.concatenate([p.astype(BF16) for p in ps], axis=1), vh[keys, :], ((1,), (0,)))
            if start:
                ls[i] = total
                accs[i] = got
            else:
                a = jnp.exp2((before - top) * SCALE)
                ls[i] = a * ls[i] + total
                accs[i] = a * accs[i] + got

        for i in range(4):
            chunk(i, 1792 + TQ * i, TK, True)

        def back(r, _):
            for i in range(4):
                chunk(i, 1792 + TQ * i - TK * r, TK, False)
            return 0

        lax.fori_loop(1, 4, back, 0)
        for i in range(4):
            chunk(i, TQ * i, TQ, False)
            att[i * TQ : (i + 1) * TQ, at] = accs[i] / jnp.sum(ls[i], axis=1, keepdims=True)

        @pl.when(hh == 1)
        def _():
            reduce_y()

        @pl.when(hh == 3)
        def _():
            reduce_x()

        return 0

    lax.fori_loop(0, GH, head, 0)
    reduce_end()

    speed = rates[mine]
    for n in range(3):

        def square(i, s):
            g = gsum[n, pl.ds(pl.multiple_of(i * 32, 32), 32), :].astype(F32)
            return s + g * g

        total = lax.fori_loop(0, FW // 32, square, jnp.zeros((32, FW), F32))
        mean = jnp.sum(jnp.sum(total, axis=0, keepdims=True), axis=1, keepdims=True) * (1.0 / (FW * FW))
        factor = speed * lax.rsqrt(mean + 1e-6)

        def move(i, _):
            at = pl.ds(pl.multiple_of(i * HD, HD), HD)
            old = wb[n, :, at].astype(F32)
            moved = old - factor * gsum[n, :, at].astype(F32)
            kept = jnp.sqrt(jnp.sum(old * old, axis=0, keepdims=True))
            fresh = jnp.sqrt(jnp.sum(moved * moved, axis=0, keepdims=True) + 1e-6)
            new[n, :, at] = (moved * (kept / fresh)).astype(BF16)
            return 0

        lax.fori_loop(0, GH, move, 0)

    def tile(n, _):
        b = nth(7 - n, near)
        qn = normed(qb[b])
        gate = dot(qn, new[0], ((1,), (0,)))
        up = dot(qn, new[1], ((1,), (0,)))
        applied = (gate * jax.nn.sigmoid(gate) * up).astype(BF16)
        rows = pl.ds(pl.multiple_of(b * TB, TB), TB)
        mixed[b] = (dot(applied, new[2], ((1,), (0,))) + att[rows, :]).astype(BF16)
        zt, xt, ct = 2 * c + lax.div(b, 4), lax.rem(lax.div(b, 2), 2), lax.rem(b, 2)
        here = own & (b == block)

        @pl.when(here)
        def _():
            pltpu.make_async_copy(mixed.at[b], out.at[mine], r_o.at[mine]).start()

        @pl.when(jnp.logical_not(here))
        def _():
            rcopy(mixed.at[b], out.at[mine], s_o.at[b], r_o.at[mine], dev(row, zt, xt, ct)).start()

        return 0

    lax.fori_loop(0, 8, tile, 0)
    for g in range(8):
        sem_wait_bytes(mixed.at[g], r_o.at[g])

    for b in range(8):

        @pl.when(jnp.logical_not(own & (block == b)))
        def _():
            sem_wait_bytes(mixed.at[b], s_o.at[b])

    for n in range(7):
        sem_wait_bytes(w2.at[n], s_kv.at[n])
        sem_wait_bytes(qb.at[n], s_q.at[n])

    @pl.when(jnp.logical_not(own))
    def _():
        sem_wait_bytes(w2.at[7], s_kv.at[7])
        sem_wait_bytes(qb.at[7], s_q.at[7])

    @pl.when(own)
    def _():
        for n in range(3):
            sem_wait_bytes(wb.at[n], s_w.at[n])

    @pl.when(c == 0)
    def _():
        for b in range(8):
            sem_wait_bytes(w1.at[b], s_g.at[b])

    @pl.when((c == 0) & (row > 0))
    def _():
        for b in range(8):
            sem_wait_bytes(w1.at[b], s_r.at[b])

    @pl.when(jnp.logical_not(last))
    def _():
        for b in range(8):
            sem_wait_bytes(w1.at[b], s_f.at[b])

    for k in range(4):
        sem_wait_bytes(r2, s0.at[k])
        sem_wait_bytes(r2, s4.at[k])
        if k:
            sem_wait_bytes(r2, s1.at[k])
            sem_wait_bytes(r2, s3.at[k])
    sem_wait_bytes(r2, s2)


def layer(kvr, q, wg, wu, wd, rates, wins):
    dma = pltpu.SemaphoreType.DMA
    piece = (3, PART, FW)
    mats = (3, FW, FW)
    half = (8 * TB, FW)
    vmem = [
        ((8, KVR, FW), BF16),
        ((8, 2 * TB, FW), BF16),
        ((8, 2 * TB, FW), BF16),
        ((8, TB, FW), BF16),
        (mats, BF16),
        (half, BF16),
        (half, BF16),
        (half, BF16),
        ((8 * TB, 2 * FW), BF16),
        (mats, BF16),
        ((4,) + piece, BF16),
        ((4,) + piece, BF16),
        ((4,) + piece, BF16),
        (piece, F32),
        (piece, BF16),
        (piece, BF16),
        (mats, BF16),
        (mats, BF16),
        ((8 * TB, HD), F32),
        ((3072, HD), BF16),
        ((3072, HD), BF16),
        ((4, TQ, HD), F32),
        ((4, TQ, HD), F32),
        ((4, TQ, HD), F32),
        (half, F32),
        ((8, TB, FW), BF16),
    ]
    d4, d8, d3 = dma((4,)), dma((8,)), dma((3,))
    sems = [d3, d8, d8, d8, d8, d8, d3, d8, d8, d8, d8, d3, d4, d4, d4, d4, dma, dma, d4, d4, d4, d4, d8, d8]
    smem = pl.BlockSpec(memory_space=pltpu.SMEM)
    return pl.pallas_call(
        layer_kernel,
        in_specs=[ANY] * 5 + [smem] * 2,
        out_specs=ANY,
        out_shape=jax.ShapeDtypeStruct((8, TB, FW), BF16),
        scratch_shapes=[pltpu.VMEM(s, d) for s, d in vmem] + sems,
        compiler_params=pltpu.CompilerParams(
            collective_id=0, has_side_effects=True, vmem_limit_bytes=60 * 1024 * 1024
        ),
        name="layer",
    )(kvr, q, wg, wu, wd, rates, wins)


def restore_kernel(order, a, o):
    for g in range(8):
        for j in range(GH):
            at = pl.ds(pl.multiple_of(order[g * GH + j] * HD, HD), HD)
            o[:, at] = a[g, :, j * HD : (j + 1) * HD]


def restore(order, a):
    return pl.pallas_call(
        restore_kernel,
        grid_spec=pltpu.PrefetchScalarGridSpec(
            num_scalar_prefetch=1,
            grid=(4,),
            in_specs=[pl.BlockSpec((8, TB // 4, FW), lambda i, o: (0, i, 0))],
            out_specs=pl.BlockSpec((TB // 4, 40 * HD), lambda i, o: (i, 0)),
        ),
        out_shape=jax.ShapeDtypeStruct((TB, 40 * HD), BF16),
        name="restore",
    )(order, a)


def per_device(queries, keys, values, step_rate, doc_start, window_len, head_order, learn_rate, w_gate, w_up, w_down):
    doc = lax.dynamic_slice_in_dim(doc_start, lax.axis_index("head") * TB, TB)
    line = lax.broadcasted_iota(jnp.int32, (8, 16, TB), 1)
    digits = jnp.where(line == 1, (doc // TB)[None, None, :], (doc % TB)[None, None, :]).astype(BF16)
    extra = jnp.where(line == 0, step_rate.T[:, None, :], digits)
    kvr, q = reorder(head_order, queries, keys, values, extra)
    mixed = layer(kvr, q, w_gate, w_up, w_down, learn_rate, window_len[head_order])
    return restore(head_order, mixed)


def solution(mesh):
    both = P(("seq", "head"), None)
    placed = (both, both, both, both, P("seq"), P(), P(), P()) + (P("head", None, None),) * 3
    return jax.shard_map(per_device, mesh=mesh, in_specs=placed, out_specs=both, check_vma=False)
```

```python
import functools

import jax
import jax.numpy as jnp
from jax import lax
from jax.experimental import pallas as pl
from jax.experimental.pallas import tpu as pltpu
from jax.sharding import PartitionSpec as P

MESH = pl.DeviceIdType.MESH
ANY = pl.BlockSpec(memory_space=pl.ANY)
VM = pl.BlockSpec(memory_space=pltpu.VMEM)
HD = 128
GH = 5
FW = 640
TB = 128
KVR = 272
ROWS = 8
F32 = jnp.float32
BF16 = jnp.bfloat16

SEND_ORDER = ((0, 1), (1, 0), (3, 0), (2, 1), (1, 1), (2, 0), (3, 1))
WAVES = ((0, 1, 2, 4), (3, 5, 6))


def coords():
    s, h = lax.axis_index("seq"), lax.axis_index("head")
    return lax.div(s, 4), lax.rem(s, 4), lax.div(h, 2), lax.rem(h, 2)


def dev(row, z, x, c):
    return (row * 4 + z, x * 2 + c)


def sem_wait_bytes(ref, sem):
    pltpu.make_async_copy(ref, ref, sem).wait()


def signal(sem, device):
    pl.semaphore_signal(sem, inc=1, device_id=device, device_id_type=MESH)


def rcopy(src, dst, ssem, rsem, device):
    return pltpu.make_async_remote_copy(
        src_ref=src, dst_ref=dst, send_sem=ssem, recv_sem=rsem, device_id=device, device_id_type=MESH
    )


def reorder_kernel(order, q, k, v, rate, kvr, qo):
    g = pl.program_id(0)
    for j in range(GH):
        at = pl.ds(pl.multiple_of(order[g * GH + j] * HD, HD), HD)
        to = slice(j * HD, (j + 1) * HD)
        kvr[0, 0:TB, to] = k[:, at]
        kvr[0, TB : 2 * TB, to] = v[:, at]
        qo[0, :, to] = q[:, at]
    kvr[0, 2 * TB :, 0:HD] = rate[0]
    kvr[0, 2 * TB :, HD:] = jnp.zeros((KVR - 2 * TB, FW - HD), BF16)


def reorder(head_order, q, k, v, rate):
    whole = pl.BlockSpec((TB, 40 * HD), lambda g, o: (0, 0))
    return pl.pallas_call(
        reorder_kernel,
        grid_spec=pltpu.PrefetchScalarGridSpec(
            num_scalar_prefetch=1,
            grid=(8,),
            in_specs=[whole, whole, whole, pl.BlockSpec((1, 16, HD), lambda g, o: (g, 0, 0))],
            out_specs=[
                pl.BlockSpec((1, KVR, FW), lambda g, o: (g, 0, 0)),
                pl.BlockSpec((1, TB, FW), lambda g, o: (g, 0, 0)),
            ],
        ),
        out_shape=[
            jax.ShapeDtypeStruct((8, KVR, FW), BF16),
            jax.ShapeDtypeStruct((8, TB, FW), BF16),
        ],
        name="reorder",
    )(head_order, q, k, v, rate)

SCALE = HD**-0.5 * 1.4426950408889634
TQ = 256
TK = 512
HALF = FW // 2
PART = FW // 8
LOW = -1e30


def dot(a, b, dims):
    return lax.dot_general(a, b, (dims, ((), ())), preferred_element_type=F32)


def normed(x):
    x = x.astype(F32)
    return (x * lax.rsqrt(jnp.mean(x * x, axis=-1, keepdims=True) + 1e-6)).astype(BF16)


def column(row):
    return jnp.broadcast_to(row, (TB, TB)).T


def layer_kernel(
    kvr, q, wg, wu, wd, rates, wins, out,
    w2, w1, w0, qb, wb, kn, hid, tgt, bgu, grad, r0, h, r1, tot, part, r2, gsum, new, docs, kh, vh, ms, ls, accs, att, mixed, rb,
    s_l, s_kv, s_q, s_f, s_g, s_r, s_w, r_kv, r_q, r_w0, r_w1, r_w, s0, t0, s1, t1, s2, t2, s3, t3, s4, t4, s_o, r_o, s_rb, r_rb,
):
    row, z, x, c = coords()
    half = lax.div(z, 2)
    block = lax.rem(z, 2) * 4 + x * 2 + c
    own = half == c
    mine = 4 * x + z
    y, xh = lax.rem(row, 4), lax.div(row, 4)
    partner = dev(row, z, x, 1 - c)
    across = dev((1 - xh) * 4 + y, z, x, c)
    peer = lambda k: lax.rem(y + k, 4)
    peer_dev = lambda k: dev(xh * 4 + peer(k), z, x, c)
    last = row == ROWS - 1
    one = lambda p: p.astype(jnp.int32)

    barrier = pltpu.get_barrier_semaphore()
    for dz in range(4):
        for dx in range(2):
            for dc in range(2):
                if dz or dx or dc:
                    signal(barrier, dev(row, lax.rem(z + dz, 4), lax.rem(x + dx, 2), lax.rem(c + dc, 2)))
    for k in (1, 2, 3):
        signal(barrier, peer_dev(k))
    signal(barrier, across)

    @pl.when((c == 0) & (row > 0))
    def _():
        signal(barrier, dev(row - 1, z, x, 0))
        signal(barrier, dev(row - 1, z, x, 1))

    @pl.when(row == 7)
    def _():
        signal(barrier, dev(3, z, 1 - x, c))

    @pl.when((row == 4) & (c == 0))
    def _():
        signal(barrier, dev(0, z, x, 1))
        signal(barrier, dev(7, z, 1 - x, 0))
        signal(barrier, dev(7, z, 1 - x, 1))

    carrier = (row == 0) | (row == 7)

    @pl.when(own)
    def _():
        pltpu.make_async_copy(kvr.at[mine], w2.at[block], r_kv.at[block]).start()
        pltpu.make_async_copy(q.at[mine], qb.at[block], r_q.at[block]).start()
        for n, w in enumerate((wg, wu, wd)):
            pltpu.make_async_copy(w.at[lax.rem(z, 2)], wb.at[n], r_w.at[n]).start()

    @pl.when(row == 0)
    def _():
        w0[...] = jnp.zeros_like(w0)

    @pl.when((row == 0) & (c == 0))
    def _():
        w1[...] = jnp.zeros_like(w1)

    pl.semaphore_wait(barrier, 19 + one(jnp.logical_not(last)) + one(row == 3) + one((row == 0) & (c == 1)) + one(last))

    def target(dz, dx):
        zt, xt = lax.rem(z + dz, 4), lax.rem(x + dx, 2)
        return 4 * xt + zt, dev(row, zt, xt, half)

    @pl.when(jnp.logical_not(own))
    def _():
        rcopy(kvr.at[mine], w2.at[block], s_kv.at[7], r_kv.at[block], partner).start()

    def wave(w):
        for n in WAVES[w]:
            g, to = target(*SEND_ORDER[n])
            rcopy(kvr.at[g], w2.at[block], s_kv.at[n], r_kv.at[block], to).start()

    wave(0)

    @pl.when(own)
    def _():
        for n, w in enumerate((wg, wu, wd)):
            rcopy(w.at[lax.rem(z, 2)], wb.at[n], s_w.at[n], r_w.at[n], partner).start()

    for n in range(3):
        sem_wait_bytes(wb.at[n], r_w.at[n])

    def nth(n, local, z_first, x=x):
        p = lax.div(n, 2)
        zs = lax.rem(z_first + jnp.where(local, lax.div(p, 2), lax.rem(lax.div(p + 1, 2), 2)), 2)
        return zs * 4 + lax.rem(x + p, 2) * 2 + lax.rem(n, 2)

    near = jnp.where(own, lax.rem(z, 2), jnp.where(z == 0, 1, jnp.where(z == 3, 0, 1 - lax.rem(z, 2))))

    def arrive(n, _):
        @pl.when(n == 2 * one(own))
        def _():
            for k in WAVES[0]:
                sem_wait_bytes(w2.at[k], s_kv.at[k])
            wave(1)

        b = nth(n, own, near)
        sem_wait_bytes(w2.at[b], r_kv.at[b])
        kv = w2.at[b, pl.ds(0, 2 * TB)]

        direct = jnp.logical_not(last) & ((row != 3) | (n >= 6))

        @pl.when(direct & (c == 0))
        def _():
            rcopy(kv, w0.at[b], s_f.at[b], r_w0.at[b], dev(row + 1, z, x, 0)).start()

        @pl.when(direct & (c == 1))
        def _():
            rcopy(kv, w1.at[b], s_f.at[b], r_w1.at[b], dev(row + 1, z, x, 0)).start()

        @pl.when((row == 3) & (n < 3))
        def _():
            rcopy(kv, rb.at[n], s_f.at[b], r_rb.at[n], dev(0, z, x, c)).start()

        @pl.when((row == 3) & (n >= 3) & (n < 6))
        def _():
            rcopy(kv, rb.at[n - 3], s_f.at[b], r_rb.at[n - 3], dev(7, z, 1 - x, c)).start()

        @pl.when(c == 0)
        def _():
            rcopy(kv, w1.at[b], s_g.at[b], r_w1.at[b], partner).start()

        rows = pl.ds(pl.multiple_of(b * TB, TB), TB)
        k = normed(w2[b, 0:TB, :])
        kn[rows, :] = k
        extra = w2[b, 2 * TB : KVR, 0:HD].astype(F32)
        docs[rows, :] = column(extra[1:2]) * float(TB) + column(extra[2:3])
        rate = column(extra[0:1])
        for j in range(GH):
            at = slice(j * HD, (j + 1) * HD)
            tgt[rows, at] = (rate * w2[b, TB : 2 * TB, at].astype(F32)).astype(BF16)
        pre_gate = dot(k, wb[0], ((1,), (0,)))
        pre_up = dot(k, wb[1], ((1,), (0,)))
        back = -dot(tgt[rows, :], wb[2], ((1,), (1,)))
        sig = jax.nn.sigmoid(pre_gate)
        lifted = pre_gate * sig
        hid[rows, :] = (lifted * pre_up).astype(BF16)
        bgu[rows, 0:FW] = (back * pre_up * sig * (1.0 + pre_gate * (1.0 - sig))).astype(BF16)
        bgu[rows, FW:] = (back * lifted).astype(BF16)
        return 0

    lax.fori_loop(0, 8, arrive, 0)

    @pl.when(carrier)
    def _():
        for m in range(3):
            far = row == 7
            xs = jnp.where(far, 1 - x, x)
            b = nth(m + 3 * one(far), own, near, xs)
            sem_wait_bytes(rb.at[m], r_rb.at[m])

            @pl.when(c == 0)
            def _():
                rcopy(rb.at[m], w0.at[b], s_rb.at[m], r_w0.at[b], dev(4, z, xs, 0)).start()

            @pl.when(c == 1)
            def _():
                rcopy(rb.at[m], w1.at[b], s_rb.at[m], r_w1.at[b], dev(4, z, xs, 0)).start()

    for k in WAVES[1]:
        sem_wait_bytes(w2.at[k], s_kv.at[k])
    for n, (dz, dx) in enumerate(SEND_ORDER):
        g, to = target(dz, dx)
        rcopy(q.at[g], qb.at[block], s_q.at[n], r_q.at[block], to).start()

    @pl.when(jnp.logical_not(own))
    def _():
        rcopy(q.at[mine], qb.at[block], s_q.at[7], r_q.at[block], partner).start()

    def grad_rows(i, _):
        at = pl.ds(pl.multiple_of(i * HD, HD), HD)
        both = dot(kn[:, at], bgu[...], ((0,), (0,)))
        grad[0, at, :] = both[:, 0:FW].astype(BF16)
        grad[1, at, :] = both[:, FW:].astype(BF16)
        grad[2, at, :] = (-dot(hid[:, at], tgt[...], ((0,), (0,)))).astype(BF16)
        return 0

    lax.fori_loop(0, GH, grad_rows, 0)

    rows_of = lambda core, k: pl.ds(pl.multiple_of(core * HALF + peer(k) * PART, 16), PART)
    order = (2, 1, 3, 0)
    for k in order:
        rcopy(grad.at[:, rows_of(1 - c, k), :], r0.at[k], s0.at[k], t0.at[k], partner).start()
    for k in order:
        sem_wait_bytes(r0.at[k], t0.at[k])
        total = grad[:, rows_of(c, k), :].astype(F32) + r0[k].astype(F32)
        if k:
            h[k] = total.astype(BF16)
            rcopy(h.at[k], r1.at[4 - k], s1.at[k], t1.at[4 - k], peer_dev(k)).start()
        else:
            tot[...] = total

    def reduce_y():
        for k in (1, 3, 2):
            sem_wait_bytes(r1.at[k], t1.at[k])
        total = tot[...] + r1[1].astype(F32) + r1[2].astype(F32) + r1[3].astype(F32)
        part[...] = total.astype(BF16)
        rcopy(part, r2, s2, t2, across).start()

    def reduce_x():
        sem_wait_bytes(r2, t2)
        at = rows_of(c, 0)
        gsum[:, at, :] = (part[...].astype(F32) + r2[...].astype(F32)).astype(BF16)
        done = gsum.at[:, at, :]
        for k in (2, 1, 3):
            rcopy(done, done, s3.at[k], t3.at[4 - k], peer_dev(k)).start()
        rcopy(done, done, s4.at[0], t4.at[y], partner).start()

    def reduce_end():
        for k in (1, 3, 2):
            got = gsum.at[:, rows_of(c, k), :]
            sem_wait_bytes(r2, t3.at[k])
            rcopy(got, got, s4.at[k], t4.at[peer(k)], partner).start()
        for k in range(4):
            sem_wait_bytes(r2, t4.at[k])

    @pl.when((c == 0) & (row > 0))
    def _():
        def relay(n, _):
            b = nth(n, half == 1, jnp.where(half == 1, lax.rem(z, 2), 1 - z))
            sem_wait_bytes(w1.at[b], r_w1.at[b])
            rcopy(w1.at[b], w0.at[b], s_r.at[b], r_w0.at[b], partner).start()
            return 0

        lax.fori_loop(0, 8, relay, 0)

    @pl.when(row > 0)
    def _():
        for b in range(8):
            sem_wait_bytes(w0.at[b], r_w0.at[b])

    @pl.when(c == 1)
    def _():
        for b in range(8):
            sem_wait_bytes(w1.at[b], r_w1.at[b])

    for b in range(8):
        sem_wait_bytes(qb.at[b], r_q.at[b])

    base = (row * 2048 + c * 1024 - 2048).astype(F32)
    lane = lax.broadcasted_iota(jnp.int32, (TQ, HD), 1).astype(F32)
    down = lax.broadcasted_iota(jnp.int32, (TQ, HD), 0).astype(F32)

    def head(hh, _):
        at = pl.ds(pl.multiple_of(hh * HD, HD), HD)
        win = wins[mine * GH + hh].astype(F32)
        for n, w in enumerate((w0, w1, w2)):
            for b in range(8):
                rows = slice(n * 1024 + b * TB, n * 1024 + (b + 1) * TB)
                kh[rows, :] = w[b, 0:TB, at]
                vh[rows, :] = w[b, TB : 2 * TB, at]

        def chunk(i, first, width, start):
            keys = pl.ds(first if isinstance(first, int) else pl.multiple_of(first, TQ), width)
            qt = qb[2 * i : 2 * i + 2, :, at].reshape(TQ, HD)
            s = dot(qt, kh[keys, :], ((1,), (1,)))
            off = first.astype(F32) if not isinstance(first, int) else float(first)
            low = jnp.maximum(docs[i * TQ : (i + 1) * TQ, :] - base, down + (2049.0 + TQ * i) - win) - off
            parts = []
            for t in range(width // HD):
                seen = lane >= low - float(HD * t)
                if start:
                    seen = seen & (lane <= down + float(width - TQ - HD * t))
                parts.append(jnp.where(seen, s[:, t * HD : (t + 1) * HD], LOW))
            top = functools.reduce(jnp.maximum, parts)
            top = jnp.broadcast_to(jnp.max(top, axis=1, keepdims=True), (TQ, HD))
            if not start:
                before = ms[i]
                top = jnp.maximum(before, top)
            ms[i] = top
            ps = [jnp.exp2((p - top) * SCALE) for p in parts]
            total = functools.reduce(jnp.add, ps)
            got = dot(jnp.concatenate([p.astype(BF16) for p in ps], axis=1), vh[keys, :], ((1,), (0,)))
            if start:
                ls[i] = total
                accs[i] = got
            else:
                a = jnp.exp2((before - top) * SCALE)
                ls[i] = a * ls[i] + total
                accs[i] = a * accs[i] + got

        for i in range(4):
            chunk(i, 1792 + TQ * i, TK, True)

        def back(r, _):
            for i in range(4):
                chunk(i, 1792 + TQ * i - TK * r, TK, False)
            return 0

        lax.fori_loop(1, 4, back, 0)
        for i in range(4):
            chunk(i, TQ * i, TQ, False)
            att[i * TQ : (i + 1) * TQ, at] = accs[i] / jnp.sum(ls[i], axis=1, keepdims=True)

        @pl.when(hh == 1)
        def _():
            reduce_y()

        @pl.when(hh == 3)
        def _():
            reduce_x()

        return 0

    lax.fori_loop(0, GH, head, 0)
    reduce_end()

    speed = rates[mine]
    for n in range(3):

        def square(i, s):
            g = gsum[n, pl.ds(pl.multiple_of(i * 32, 32), 32), :].astype(F32)
            return s + g * g

        total = lax.fori_loop(0, FW // 32, square, jnp.zeros((32, FW), F32))
        mean = jnp.sum(jnp.sum(total, axis=0, keepdims=True), axis=1, keepdims=True) * (1.0 / (FW * FW))
        factor = speed * lax.rsqrt(mean + 1e-6)

        def move(i, _):
            at = pl.ds(pl.multiple_of(i * HD, HD), HD)
            old = wb[n, :, at].astype(F32)
            moved = old - factor * gsum[n, :, at].astype(F32)
            kept = jnp.sqrt(jnp.sum(old * old, axis=0, keepdims=True))
            fresh = jnp.sqrt(jnp.sum(moved * moved, axis=0, keepdims=True) + 1e-6)
            new[n, :, at] = (moved * (kept / fresh)).astype(BF16)
            return 0

        lax.fori_loop(0, GH, move, 0)

    def tile(n, _):
        b = nth(7 - n, own, near)
        qn = normed(qb[b])
        gate = dot(qn, new[0], ((1,), (0,)))
        up = dot(qn, new[1], ((1,), (0,)))
        applied = (gate * jax.nn.sigmoid(gate) * up).astype(BF16)
        rows = pl.ds(pl.multiple_of(b * TB, TB), TB)
        mixed[b] = (dot(applied, new[2], ((1,), (0,))) + att[rows, :]).astype(BF16)
        zt, xt, ct = 2 * c + lax.div(b, 4), lax.rem(lax.div(b, 2), 2), lax.rem(b, 2)
        here = own & (b == block)

        @pl.when(here)
        def _():
            pltpu.make_async_copy(mixed.at[b], out.at[mine], r_o.at[mine]).start()

        @pl.when(jnp.logical_not(here))
        def _():
            rcopy(mixed.at[b], out.at[mine], s_o.at[b], r_o.at[mine], dev(row, zt, xt, ct)).start()

        return 0

    lax.fori_loop(0, 8, tile, 0)
    for g in range(8):
        sem_wait_bytes(mixed.at[g], r_o.at[g])

    @pl.when(carrier)
    def _():
        for m in range(3):
            sem_wait_bytes(rb.at[m], s_rb.at[m])

    for b in range(8):

        @pl.when(jnp.logical_not(own & (block == b)))
        def _():
            sem_wait_bytes(mixed.at[b], s_o.at[b])

    for n in range(7):
        sem_wait_bytes(qb.at[n], s_q.at[n])

    @pl.when(jnp.logical_not(own))
    def _():
        sem_wait_bytes(w2.at[7], s_kv.at[7])
        sem_wait_bytes(qb.at[7], s_q.at[7])

    @pl.when(own)
    def _():
        for n in range(3):
            sem_wait_bytes(wb.at[n], s_w.at[n])

    @pl.when(c == 0)
    def _():
        for b in range(8):
            sem_wait_bytes(w1.at[b], s_g.at[b])

    @pl.when((c == 0) & (row > 0))
    def _():
        for b in range(8):
            sem_wait_bytes(w1.at[b], s_r.at[b])

    @pl.when(jnp.logical_not(last))
    def _():
        for b in range(8):
            sem_wait_bytes(w1.at[b], s_f.at[b])

    for k in range(4):
        sem_wait_bytes(r2, s0.at[k])
        sem_wait_bytes(r2, s4.at[k])
        if k:
            sem_wait_bytes(r2, s1.at[k])
            sem_wait_bytes(r2, s3.at[k])
    sem_wait_bytes(r2, s2)


def layer(kvr, q, wg, wu, wd, rates, wins):
    dma = pltpu.SemaphoreType.DMA
    piece = (3, PART, FW)
    mats = (3, FW, FW)
    half = (8 * TB, FW)
    vmem = [
        ((8, KVR, FW), BF16),
        ((8, 2 * TB, FW), BF16),
        ((8, 2 * TB, FW), BF16),
        ((8, TB, FW), BF16),
        (mats, BF16),
        (half, BF16),
        (half, BF16),
        (half, BF16),
        ((8 * TB, 2 * FW), BF16),
        (mats, BF16),
        ((4,) + piece, BF16),
        ((4,) + piece, BF16),
        ((4,) + piece, BF16),
        (piece, F32),
        (piece, BF16),
        (piece, BF16),
        (mats, BF16),
        (mats, BF16),
        ((8 * TB, HD), F32),
        ((3072, HD), BF16),
        ((3072, HD), BF16),
        ((4, TQ, HD), F32),
        ((4, TQ, HD), F32),
        ((4, TQ, HD), F32),
        (half, F32),
        ((8, TB, FW), BF16),
        ((3, 2 * TB, FW), BF16),
    ]
    d4, d8, d3 = dma((4,)), dma((8,)), dma((3,))
    sems = [d3, d8, d8, d8, d8, d8, d3, d8, d8, d8, d8, d3, d4, d4, d4, d4, dma, dma, d4, d4, d4, d4, d8, d8, d3, d3]
    smem = pl.BlockSpec(memory_space=pltpu.SMEM)
    return pl.pallas_call(
        layer_kernel,
        in_specs=[ANY] * 5 + [smem] * 2,
        out_specs=ANY,
        out_shape=jax.ShapeDtypeStruct((8, TB, FW), BF16),
        scratch_shapes=[pltpu.VMEM(s, d) for s, d in vmem] + sems,
        compiler_params=pltpu.CompilerParams(
            collective_id=0, has_side_effects=True, vmem_limit_bytes=60 * 1024 * 1024
        ),
        name="layer",
    )(kvr, q, wg, wu, wd, rates, wins)


def restore_kernel(order, a, o):
    for g in range(8):
        for j in range(GH):
            at = pl.ds(pl.multiple_of(order[g * GH + j] * HD, HD), HD)
            o[:, at] = a[g, :, j * HD : (j + 1) * HD]


def restore(order, a):
    return pl.pallas_call(
        restore_kernel,
        grid_spec=pltpu.PrefetchScalarGridSpec(
            num_scalar_prefetch=1,
            grid=(4,),
            in_specs=[pl.BlockSpec((8, TB // 4, FW), lambda i, o: (0, i, 0))],
            out_specs=pl.BlockSpec((TB // 4, 40 * HD), lambda i, o: (i, 0)),
        ),
        out_shape=jax.ShapeDtypeStruct((TB, 40 * HD), BF16),
        name="restore",
    )(order, a)


def per_device(queries, keys, values, step_rate, doc_start, window_len, head_order, learn_rate, w_gate, w_up, w_down):
    doc = lax.dynamic_slice_in_dim(doc_start, lax.axis_index("head") * TB, TB)
    line = lax.broadcasted_iota(jnp.int32, (8, 16, TB), 1)
    digits = jnp.where(line == 1, (doc // TB)[None, None, :], (doc % TB)[None, None, :]).astype(BF16)
    extra = jnp.where(line == 0, step_rate.T[:, None, :], digits)
    kvr, q = reorder(head_order, queries, keys, values, extra)
    mixed = layer(kvr, q, w_gate, w_up, w_down, learn_rate, window_len[head_order])
    return restore(head_order, mixed)


def solution(mesh):
    both = P(("seq", "head"), None)
    placed = (both, both, both, both, P("seq"), P(), P(), P()) + (P("head", None, None),) * 3
    return jax.shard_map(per_device, mesh=mesh, in_specs=placed, out_specs=both, check_vma=False)
```

```python
import functools

import jax
import jax.numpy as jnp
from jax import lax
from jax.experimental import pallas as pl
from jax.experimental.pallas import tpu as pltpu
from jax.sharding import PartitionSpec as P

MESH = pl.DeviceIdType.MESH
ANY = pl.BlockSpec(memory_space=pl.ANY)
VM = pl.BlockSpec(memory_space=pltpu.VMEM)
HD = 128
GH = 5
FW = 640
TB = 128
KVR = 272
ROWS = 8
F32 = jnp.float32
BF16 = jnp.bfloat16

SEND_ORDER = ((0, 1), (1, 0), (3, 0), (2, 1), (1, 1), (2, 0), (3, 1))
WAVES = ((0, 1, 2, 4), (3, 5, 6))


def coords():
    s, h = lax.axis_index("seq"), lax.axis_index("head")
    return lax.div(s, 4), lax.rem(s, 4), lax.div(h, 2), lax.rem(h, 2)


def dev(row, z, x, c):
    return (row * 4 + z, x * 2 + c)


def sem_wait_bytes(ref, sem):
    pltpu.make_async_copy(ref, ref, sem).wait()


def signal(sem, device):
    pl.semaphore_signal(sem, inc=1, device_id=device, device_id_type=MESH)


def rcopy(src, dst, ssem, rsem, device):
    return pltpu.make_async_remote_copy(
        src_ref=src, dst_ref=dst, send_sem=ssem, recv_sem=rsem, device_id=device, device_id_type=MESH
    )


SCALE = HD**-0.5 * 1.4426950408889634
TQ = 256
TK = 512
HALF = FW // 2
PART = FW // 8
LOW = -1e30


def dot(a, b, dims):
    return lax.dot_general(a, b, (dims, ((), ())), preferred_element_type=F32)


def normed(x):
    x = x.astype(F32)
    return (x * lax.rsqrt(jnp.mean(x * x, axis=-1, keepdims=True) + 1e-6)).astype(BF16)


def column(row):
    return jnp.broadcast_to(row, (TB, TB)).T


def layer_kernel(
    qi, ki, vi, wg, wu, wd, extra, order_of, rates, window, out,
    qin, kin, vin, kvr, q, w2, w1, w0, qb, wb, kn, hid, tgt, bgu, grad, r0, h, r1, tot, part, r2, gsum, new, docs, kh, vh, ms, ls, accs, att, mixed, rb,
    s_l, s_kv, s_q, s_f, s_g, s_r, s_w, r_kv, r_q, r_w0, r_w1, r_w, s0, t0, s1, t1, s2, t2, s3, t3, s4, t4, s_o, r_o, s_rb, r_rb,
):
    row, z, x, c = coords()
    half = lax.div(z, 2)
    block = lax.rem(z, 2) * 4 + x * 2 + c
    own = half == c
    mine = 4 * x + z
    y, xh = lax.rem(row, 4), lax.div(row, 4)
    partner = dev(row, z, x, 1 - c)
    across = dev((1 - xh) * 4 + y, z, x, c)
    peer = lambda k: lax.rem(y + k, 4)
    peer_dev = lambda k: dev(xh * 4 + peer(k), z, x, c)
    last = row == ROWS - 1
    one = lambda p: p.astype(jnp.int32)

    for n, (a, b) in enumerate(((ki, kin), (vi, vin), (qi, qin))):

        def fetch(i, _):
            at = pl.ds(pl.multiple_of(i * HD, HD), HD)
            pltpu.make_async_copy(a.at[:, at], b.at[i], s_l.at[n]).start()
            return 0

        lax.fori_loop(0, 8 * GH, fetch, 0)

    barrier = pltpu.get_barrier_semaphore()
    for dz in range(4):
        for dx in range(2):
            for dc in range(2):
                if dz or dx or dc:
                    signal(barrier, dev(row, lax.rem(z + dz, 4), lax.rem(x + dx, 2), lax.rem(c + dc, 2)))
    for k in (1, 2, 3):
        signal(barrier, peer_dev(k))
    signal(barrier, across)

    @pl.when((c == 0) & (row > 0))
    def _():
        signal(barrier, dev(row - 1, z, x, 0))
        signal(barrier, dev(row - 1, z, x, 1))

    @pl.when(row == 7)
    def _():
        signal(barrier, dev(3, z, 1 - x, c))

    @pl.when((row == 4) & (c == 0))
    def _():
        signal(barrier, dev(0, z, x, 1))
        signal(barrier, dev(7, z, 1 - x, 0))
        signal(barrier, dev(7, z, 1 - x, 1))

    carrier = (row == 0) | (row == 7)

    def stage_kv(g, _):
        kvr[g, 2 * TB : KVR, :] = jnp.zeros((KVR - 2 * TB, FW), BF16)
        kvr[g, 2 * TB : KVR, 0:HD] = extra[g]
        for j in range(GH):
            to = slice(j * HD, (j + 1) * HD)
            kvr[g, 0:TB, to] = kin[order_of[g * GH + j]]
            kvr[g, TB : 2 * TB, to] = vin[order_of[g * GH + j]]
        return 0

    def stage_q(g, _):
        for j in range(GH):
            q[g, :, j * HD : (j + 1) * HD] = qin[order_of[g * GH + j]]
        return 0

    sem_wait_bytes(kin, s_l.at[0])
    sem_wait_bytes(vin, s_l.at[1])
    lax.fori_loop(0, 8, stage_kv, 0)

    @pl.when(own)
    def _():
        pltpu.make_async_copy(kvr.at[mine], w2.at[block], r_kv.at[block]).start()
        for n, w in enumerate((wg, wu, wd)):
            pltpu.make_async_copy(w.at[lax.rem(z, 2)], wb.at[n], r_w.at[n]).start()

    @pl.when(row == 0)
    def _():
        w0[...] = jnp.zeros_like(w0)

    @pl.when((row == 0) & (c == 0))
    def _():
        w1[...] = jnp.zeros_like(w1)

    pl.semaphore_wait(barrier, 19 + one(jnp.logical_not(last)) + one(row == 3) + one((row == 0) & (c == 1)) + one(last))

    def target(dz, dx):
        zt, xt = lax.rem(z + dz, 4), lax.rem(x + dx, 2)
        return 4 * xt + zt, dev(row, zt, xt, half)

    @pl.when(jnp.logical_not(own))
    def _():
        rcopy(kvr.at[mine], w2.at[block], s_kv.at[7], r_kv.at[block], partner).start()

    def wave(w):
        for n in WAVES[w]:
            g, to = target(*SEND_ORDER[n])
            rcopy(kvr.at[g], w2.at[block], s_kv.at[n], r_kv.at[block], to).start()

    wave(0)

    @pl.when(own)
    def _():
        for n, w in enumerate((wg, wu, wd)):
            rcopy(w.at[lax.rem(z, 2)], wb.at[n], s_w.at[n], r_w.at[n], partner).start()

    sem_wait_bytes(qin, s_l.at[2])
    lax.fori_loop(0, 8, stage_q, 0)

    @pl.when(own)
    def _():
        pltpu.make_async_copy(q.at[mine], qb.at[block], r_q.at[block]).start()

    for n in range(3):
        sem_wait_bytes(wb.at[n], r_w.at[n])

    def nth(n, local, z_first, x=x):
        p = lax.div(n, 2)
        zs = lax.rem(z_first + jnp.where(local, lax.div(p, 2), lax.rem(lax.div(p + 1, 2), 2)), 2)
        return zs * 4 + lax.rem(x + p, 2) * 2 + lax.rem(n, 2)

    near = jnp.where(own, lax.rem(z, 2), jnp.where(z == 0, 1, jnp.where(z == 3, 0, 1 - lax.rem(z, 2))))

    def arrive(n, _):
        @pl.when(n == 2 * one(own))
        def _():
            for k in WAVES[0]:
                sem_wait_bytes(w2.at[k], s_kv.at[k])
            wave(1)

        b = nth(n, own, near)
        sem_wait_bytes(w2.at[b], r_kv.at[b])
        kv = w2.at[b, pl.ds(0, 2 * TB)]

        direct = jnp.logical_not(last) & ((row != 3) | (n >= 6))

        @pl.when(direct & (c == 0))
        def _():
            rcopy(kv, w0.at[b], s_f.at[b], r_w0.at[b], dev(row + 1, z, x, 0)).start()

        @pl.when(direct & (c == 1))
        def _():
            rcopy(kv, w1.at[b], s_f.at[b], r_w1.at[b], dev(row + 1, z, x, 0)).start()

        @pl.when((row == 3) & (n < 3))
        def _():
            rcopy(kv, rb.at[n], s_f.at[b], r_rb.at[n], dev(0, z, x, c)).start()

        @pl.when((row == 3) & (n >= 3) & (n < 6))
        def _():
            rcopy(kv, rb.at[n - 3], s_f.at[b], r_rb.at[n - 3], dev(7, z, 1 - x, c)).start()

        @pl.when(c == 0)
        def _():
            rcopy(kv, w1.at[b], s_g.at[b], r_w1.at[b], partner).start()

        rows = pl.ds(pl.multiple_of(b * TB, TB), TB)
        k = normed(w2[b, 0:TB, :])
        kn[rows, :] = k
        extra = w2[b, 2 * TB : KVR, 0:HD].astype(F32)
        docs[rows, :] = column(extra[1:2]) * float(TB) + column(extra[2:3])
        rate = column(extra[0:1])
        for j in range(GH):
            at = slice(j * HD, (j + 1) * HD)
            tgt[rows, at] = (rate * w2[b, TB : 2 * TB, at].astype(F32)).astype(BF16)
        pre_gate = dot(k, wb[0], ((1,), (0,)))
        pre_up = dot(k, wb[1], ((1,), (0,)))
        back = -dot(tgt[rows, :], wb[2], ((1,), (1,)))
        sig = jax.nn.sigmoid(pre_gate)
        lifted = pre_gate * sig
        hid[rows, :] = (lifted * pre_up).astype(BF16)
        bgu[rows, 0:FW] = (back * pre_up * sig * (1.0 + pre_gate * (1.0 - sig))).astype(BF16)
        bgu[rows, FW:] = (back * lifted).astype(BF16)
        return 0

    lax.fori_loop(0, 8, arrive, 0)

    @pl.when(carrier)
    def _():
        for m in range(3):
            far = row == 7
            xs = jnp.where(far, 1 - x, x)
            b = nth(m + 3 * one(far), own, near, xs)
            sem_wait_bytes(rb.at[m], r_rb.at[m])

            @pl.when(c == 0)
            def _():
                rcopy(rb.at[m], w0.at[b], s_rb.at[m], r_w0.at[b], dev(4, z, xs, 0)).start()

            @pl.when(c == 1)
            def _():
                rcopy(rb.at[m], w1.at[b], s_rb.at[m], r_w1.at[b], dev(4, z, xs, 0)).start()

    for k in WAVES[1]:
        sem_wait_bytes(w2.at[k], s_kv.at[k])
    def grad_rows(i, _):
        at = pl.ds(pl.multiple_of(i * HD, HD), HD)
        both = dot(kn[:, at], bgu[...], ((0,), (0,)))
        grad[0, at, :] = both[:, 0:FW].astype(BF16)
        grad[1, at, :] = both[:, FW:].astype(BF16)
        grad[2, at, :] = (-dot(hid[:, at], tgt[...], ((0,), (0,)))).astype(BF16)
        return 0

    lax.fori_loop(0, GH, grad_rows, 0)

    rows_of = lambda core, k: pl.ds(pl.multiple_of(core * HALF + peer(k) * PART, 16), PART)
    order = (2, 1, 3, 0)
    for k in order:
        rcopy(grad.at[:, rows_of(1 - c, k), :], r0.at[k], s0.at[k], t0.at[k], partner).start()
    for k in order:
        sem_wait_bytes(r0.at[k], t0.at[k])
        total = grad[:, rows_of(c, k), :].astype(F32) + r0[k].astype(F32)
        if k:
            h[k] = total.astype(BF16)
            rcopy(h.at[k], r1.at[4 - k], s1.at[k], t1.at[4 - k], peer_dev(k)).start()
        else:
            tot[...] = total

    for n, (dz, dx) in enumerate(SEND_ORDER):
        g, to = target(dz, dx)
        rcopy(q.at[g], qb.at[block], s_q.at[n], r_q.at[block], to).start()

    @pl.when(jnp.logical_not(own))
    def _():
        rcopy(q.at[mine], qb.at[block], s_q.at[7], r_q.at[block], partner).start()

    def reduce_y():
        for k in (1, 3, 2):
            sem_wait_bytes(r1.at[k], t1.at[k])
        total = tot[...] + r1[1].astype(F32) + r1[2].astype(F32) + r1[3].astype(F32)
        part[...] = total.astype(BF16)
        rcopy(part, r2, s2, t2, across).start()

    def reduce_x():
        sem_wait_bytes(r2, t2)
        at = rows_of(c, 0)
        gsum[:, at, :] = (part[...].astype(F32) + r2[...].astype(F32)).astype(BF16)
        done = gsum.at[:, at, :]
        for k in (2, 1, 3):
            rcopy(done, done, s3.at[k], t3.at[4 - k], peer_dev(k)).start()
        rcopy(done, done, s4.at[0], t4.at[y], partner).start()

    def reduce_end():
        for k in (1, 3, 2):
            got = gsum.at[:, rows_of(c, k), :]
            sem_wait_bytes(r2, t3.at[k])
            rcopy(got, got, s4.at[k], t4.at[peer(k)], partner).start()
        for k in range(4):
            sem_wait_bytes(r2, t4.at[k])

    reduce_y()

    @pl.when((c == 0) & (row > 0))
    def _():
        def relay(n, _):
            b = nth(n, half == 1, jnp.where(half == 1, lax.rem(z, 2), 1 - z))
            sem_wait_bytes(w1.at[b], r_w1.at[b])
            rcopy(w1.at[b], w0.at[b], s_r.at[b], r_w0.at[b], partner).start()
            return 0

        lax.fori_loop(0, 8, relay, 0)

    @pl.when(row > 0)
    def _():
        for b in range(8):
            sem_wait_bytes(w0.at[b], r_w0.at[b])

    @pl.when(c == 1)
    def _():
        for b in range(8):
            sem_wait_bytes(w1.at[b], r_w1.at[b])

    for b in range(8):
        sem_wait_bytes(qb.at[b], r_q.at[b])

    base = (row * 2048 + c * 1024 - 2048).astype(F32)
    lane = lax.broadcasted_iota(jnp.int32, (TQ, HD), 1).astype(F32)
    down = lax.broadcasted_iota(jnp.int32, (TQ, HD), 0).astype(F32)

    def head(hh, _):
        at = pl.ds(pl.multiple_of(hh * HD, HD), HD)
        win = window[order_of[mine * GH + hh]].astype(F32)
        for n, w in enumerate((w0, w1, w2)):
            for b in range(8):
                rows = slice(n * 1024 + b * TB, n * 1024 + (b + 1) * TB)
                kh[rows, :] = w[b, 0:TB, at]
                vh[rows, :] = w[b, TB : 2 * TB, at]

        def chunk(i, first, width, start):
            keys = pl.ds(first if isinstance(first, int) else pl.multiple_of(first, TQ), width)
            qt = qb[2 * i : 2 * i + 2, :, at].reshape(TQ, HD)
            s = dot(qt, kh[keys, :], ((1,), (1,)))
            off = first.astype(F32) if not isinstance(first, int) else float(first)
            low = jnp.maximum(docs[i * TQ : (i + 1) * TQ, :] - base, down + (2049.0 + TQ * i) - win) - off
            parts = []
            for t in range(width // HD):
                seen = lane >= low - float(HD * t)
                if start:
                    seen = seen & (lane <= down + float(width - TQ - HD * t))
                parts.append(jnp.where(seen, s[:, t * HD : (t + 1) * HD], LOW))
            top = functools.reduce(jnp.maximum, parts)
            top = jnp.broadcast_to(jnp.max(top, axis=1, keepdims=True), (TQ, HD))
            if not start:
                before = ms[i]
                top = jnp.maximum(before, top)
            ms[i] = top
            ps = [jnp.exp2((p - top) * SCALE) for p in parts]
            total = functools.reduce(jnp.add, ps)
            got = dot(jnp.concatenate([p.astype(BF16) for p in ps], axis=1), vh[keys, :], ((1,), (0,)))
            if start:
                ls[i] = total
                accs[i] = got
            else:
                a = jnp.exp2((before - top) * SCALE)
                ls[i] = a * ls[i] + total
                accs[i] = a * accs[i] + got

        for i in range(4):
            chunk(i, 1792 + TQ * i, TK, True)

        def back(r, _):
            for i in range(4):
                chunk(i, 1792 + TQ * i - TK * r, TK, False)
            return 0

        lax.fori_loop(1, 4, back, 0)
        for i in range(4):
            chunk(i, TQ * i, TQ, False)
            att[i * TQ : (i + 1) * TQ, at] = accs[i] / jnp.sum(ls[i], axis=1, keepdims=True)

        @pl.when(hh == 1)
        def _():
            reduce_x()


        return 0

    lax.fori_loop(0, GH, head, 0)
    reduce_end()

    speed = rates[mine]
    for n in range(3):

        def square(i, s):
            g = gsum[n, pl.ds(pl.multiple_of(i * 32, 32), 32), :].astype(F32)
            return s + g * g

        total = lax.fori_loop(0, FW // 32, square, jnp.zeros((32, FW), F32))
        mean = jnp.sum(jnp.sum(total, axis=0, keepdims=True), axis=1, keepdims=True) * (1.0 / (FW * FW))
        factor = speed * lax.rsqrt(mean + 1e-6)

        def move(i, _):
            at = pl.ds(pl.multiple_of(i * HD, HD), HD)
            old = wb[n, :, at].astype(F32)
            moved = old - factor * gsum[n, :, at].astype(F32)
            kept = jnp.sqrt(jnp.sum(old * old, axis=0, keepdims=True))
            fresh = jnp.sqrt(jnp.sum(moved * moved, axis=0, keepdims=True) + 1e-6)
            new[n, :, at] = (moved * (kept / fresh)).astype(BF16)
            return 0

        lax.fori_loop(0, GH, move, 0)

    def tile(n, _):
        b = nth(7 - n, own, near)
        qn = normed(qb[b])
        gate = dot(qn, new[0], ((1,), (0,)))
        up = dot(qn, new[1], ((1,), (0,)))
        applied = (gate * jax.nn.sigmoid(gate) * up).astype(BF16)
        rows = pl.ds(pl.multiple_of(b * TB, TB), TB)
        mixed[b] = (dot(applied, new[2], ((1,), (0,))) + att[rows, :]).astype(BF16)
        zt, xt, ct = 2 * c + lax.div(b, 4), lax.rem(lax.div(b, 2), 2), lax.rem(b, 2)
        here = own & (b == block)

        @pl.when(here)
        def _():
            pltpu.make_async_copy(mixed.at[b], out.at[mine], r_o.at[mine]).start()

        @pl.when(jnp.logical_not(here))
        def _():
            rcopy(mixed.at[b], out.at[mine], s_o.at[b], r_o.at[mine], dev(row, zt, xt, ct)).start()

        return 0

    lax.fori_loop(0, 8, tile, 0)
    for g in range(8):
        sem_wait_bytes(mixed.at[g], r_o.at[g])

    @pl.when(carrier)
    def _():
        for m in range(3):
            sem_wait_bytes(rb.at[m], s_rb.at[m])

    for b in range(8):

        @pl.when(jnp.logical_not(own & (block == b)))
        def _():
            sem_wait_bytes(mixed.at[b], s_o.at[b])

    for n in range(7):
        sem_wait_bytes(qb.at[n], s_q.at[n])

    @pl.when(jnp.logical_not(own))
    def _():
        sem_wait_bytes(w2.at[7], s_kv.at[7])
        sem_wait_bytes(qb.at[7], s_q.at[7])

    @pl.when(own)
    def _():
        for n in range(3):
            sem_wait_bytes(wb.at[n], s_w.at[n])

    @pl.when(c == 0)
    def _():
        for b in range(8):
            sem_wait_bytes(w1.at[b], s_g.at[b])

    @pl.when((c == 0) & (row > 0))
    def _():
        for b in range(8):
            sem_wait_bytes(w1.at[b], s_r.at[b])

    @pl.when(jnp.logical_not(last))
    def _():
        for b in range(8):
            sem_wait_bytes(w1.at[b], s_f.at[b])

    for k in range(4):
        sem_wait_bytes(r2, s0.at[k])
        sem_wait_bytes(r2, s4.at[k])
        if k:
            sem_wait_bytes(r2, s1.at[k])
            sem_wait_bytes(r2, s3.at[k])
    sem_wait_bytes(r2, s2)


def layer(q, k, v, wg, wu, wd, extra, order, rates, window):
    dma = pltpu.SemaphoreType.DMA
    piece = (3, PART, FW)
    mats = (3, FW, FW)
    half = (8 * TB, FW)
    vmem = [
        ((8 * GH, TB, HD), BF16),
        ((8 * GH, TB, HD), BF16),
        ((8 * GH, TB, HD), BF16),
        ((8, KVR, FW), BF16),
        ((8, TB, FW), BF16),
        ((8, KVR, FW), BF16),
        ((8, 2 * TB, FW), BF16),
        ((8, 2 * TB, FW), BF16),
        ((8, TB, FW), BF16),
        (mats, BF16),
        (half, BF16),
        (half, BF16),
        (half, BF16),
        ((8 * TB, 2 * FW), BF16),
        (mats, BF16),
        ((4,) + piece, BF16),
        ((4,) + piece, BF16),
        ((4,) + piece, BF16),
        (piece, F32),
        (piece, BF16),
        (piece, BF16),
        (mats, BF16),
        (mats, BF16),
        ((8 * TB, HD), F32),
        ((3072, HD), BF16),
        ((3072, HD), BF16),
        ((4, TQ, HD), F32),
        ((4, TQ, HD), F32),
        ((4, TQ, HD), F32),
        (half, F32),
        ((8, TB, FW), BF16),
        ((3, 2 * TB, FW), BF16),
    ]
    d4, d8, d3 = dma((4,)), dma((8,)), dma((3,))
    sems = [d3, d8, d8, d8, d8, d8, d3, d8, d8, d8, d8, d3, d4, d4, d4, d4, dma, dma, d4, d4, d4, d4, d8, d8, d3, d3]
    smem = pl.BlockSpec(memory_space=pltpu.SMEM)
    return pl.pallas_call(
        layer_kernel,
        in_specs=[ANY] * 6 + [VM] + [smem] * 3,
        out_specs=ANY,
        out_shape=jax.ShapeDtypeStruct((8, TB, FW), BF16),
        scratch_shapes=[pltpu.VMEM(s, d) for s, d in vmem] + sems,
        compiler_params=pltpu.CompilerParams(
            collective_id=0, has_side_effects=True, vmem_limit_bytes=60 * 1024 * 1024
        ),
        name="layer",
    )(q, k, v, wg, wu, wd, extra, order, rates, window)


def restore_kernel(order, a, o):
    for g in range(8):
        for j in range(GH):
            at = pl.ds(pl.multiple_of(order[g * GH + j] * HD, HD), HD)
            o[:, at] = a[g, :, j * HD : (j + 1) * HD]


def restore(order, a):
    return pl.pallas_call(
        restore_kernel,
        grid_spec=pltpu.PrefetchScalarGridSpec(
            num_scalar_prefetch=1,
            grid=(4,),
            in_specs=[pl.BlockSpec((8, TB // 4, FW), lambda i, o: (0, i, 0))],
            out_specs=pl.BlockSpec((TB // 4, 40 * HD), lambda i, o: (i, 0)),
        ),
        out_shape=jax.ShapeDtypeStruct((TB, 40 * HD), BF16),
        name="restore",
    )(order, a)


def per_device(queries, keys, values, step_rate, doc_start, window_len, head_order, learn_rate, w_gate, w_up, w_down):
    doc = lax.dynamic_slice_in_dim(doc_start, lax.axis_index("head") * TB, TB)
    line = lax.broadcasted_iota(jnp.int32, (8, 16, TB), 1)
    digits = jnp.where(line == 1, (doc // TB)[None, None, :], (doc % TB)[None, None, :]).astype(BF16)
    extra = jnp.where(line == 0, step_rate.T[:, None, :], digits)
    mixed = layer(queries, keys, values, w_gate, w_up, w_down, extra, head_order, learn_rate, window_len)
    return restore(head_order, mixed)


def solution(mesh):
    both = P(("seq", "head"), None)
    placed = (both, both, both, both, P("seq"), P(), P(), P()) + (P("head", None, None),) * 3
    return jax.shard_map(per_device, mesh=mesh, in_specs=placed, out_specs=both, check_vma=False)
```

```python
import functools

import jax
import jax.numpy as jnp
from jax import lax
from jax.experimental import pallas as pl
from jax.experimental.pallas import tpu as pltpu
from jax.sharding import PartitionSpec as P

MESH = pl.DeviceIdType.MESH
ANY = pl.BlockSpec(memory_space=pl.ANY)
VM = pl.BlockSpec(memory_space=pltpu.VMEM)
HD = 128
GH = 5
FW = 640
TB = 128
KVR = 272
ROWS = 8
F32 = jnp.float32
BF16 = jnp.bfloat16

SEND_ORDER = ((0, 1), (1, 0), (3, 0), (2, 1), (1, 1), (2, 0), (3, 1))
WAVES = ((0, 1, 2), (4, 6, 5, 3))


def coords():
    s, h = lax.axis_index("seq"), lax.axis_index("head")
    return lax.div(s, 4), lax.rem(s, 4), lax.div(h, 2), lax.rem(h, 2)


def dev(row, z, x, c):
    return (row * 4 + z, x * 2 + c)


def sem_wait_bytes(ref, sem):
    pltpu.make_async_copy(ref, ref, sem).wait()


def signal(sem, device):
    pl.semaphore_signal(sem, inc=1, device_id=device, device_id_type=MESH)


def rcopy(src, dst, ssem, rsem, device):
    return pltpu.make_async_remote_copy(
        src_ref=src, dst_ref=dst, send_sem=ssem, recv_sem=rsem, device_id=device, device_id_type=MESH
    )


SCALE = HD**-0.5 * 1.4426950408889634
TQ = 256
TK = 512
HALF = FW // 2
PART = FW // 8
LOW = -1e30


def dot(a, b, dims):
    return lax.dot_general(a, b, (dims, ((), ())), preferred_element_type=F32)


def normed(x):
    x = x.astype(F32)
    return (x * lax.rsqrt(jnp.mean(x * x, axis=-1, keepdims=True) + 1e-6)).astype(BF16)


def column(row):
    return jnp.broadcast_to(row, (TB, TB)).T


def layer_kernel(
    qi, ki, vi, wg, wu, wd, extra, order_of, rates, window, out,
    qin, kin, vin, kvr, q, w2, w1, w0, qb, wb, kn, hid, tgt, bgu, grad, r0, h, r1, tot, part, r2, gsum, new, docs, kh, vh, ms, ls, accs, att, mixed, rb,
    s_l, s_kv, s_q, s_f, s_g, s_r, s_w, r_kv, r_q, r_w0, r_w1, r_w, s0, t0, s1, t1, s2, t2, s3, t3, s4, t4, s_o, r_o, s_rb, r_rb,
):
    row, z, x, c = coords()
    half = lax.div(z, 2)
    block = lax.rem(z, 2) * 4 + x * 2 + c
    own = half == c
    mine = 4 * x + z
    y, xh = lax.rem(row, 4), lax.div(row, 4)
    partner = dev(row, z, x, 1 - c)
    across = dev((1 - xh) * 4 + y, z, x, c)
    peer = lambda k: lax.rem(y + k, 4)
    peer_dev = lambda k: dev(xh * 4 + peer(k), z, x, c)
    last = row == ROWS - 1
    one = lambda p: p.astype(jnp.int32)

    for n, (a, b) in enumerate(((ki, kin), (vi, vin), (qi, qin))):

        def fetch(i, _):
            at = pl.ds(pl.multiple_of(i * HD, HD), HD)
            pltpu.make_async_copy(a.at[:, at], b.at[i], s_l.at[n]).start()
            return 0

        lax.fori_loop(0, 8 * GH, fetch, 0)

    barrier = pltpu.get_barrier_semaphore()
    for dz in range(4):
        for dx in range(2):
            for dc in range(2):
                if dz or dx or dc:
                    signal(barrier, dev(row, lax.rem(z + dz, 4), lax.rem(x + dx, 2), lax.rem(c + dc, 2)))
    for k in (1, 2, 3):
        signal(barrier, peer_dev(k))
    signal(barrier, across)

    @pl.when((c == 0) & (row > 0))
    def _():
        signal(barrier, dev(row - 1, z, x, 0))
        signal(barrier, dev(row - 1, z, x, 1))

    @pl.when(row == 7)
    def _():
        signal(barrier, dev(3, z, 1 - x, c))

    @pl.when((row == 4) & (c == 0))
    def _():
        signal(barrier, dev(0, z, x, 1))
        signal(barrier, dev(7, z, 1 - x, 0))
        signal(barrier, dev(7, z, 1 - x, 1))

    carrier = (row == 0) | (row == 7)

    def stage_kv(g, _):
        kvr[g, 2 * TB : KVR, :] = jnp.zeros((KVR - 2 * TB, FW), BF16)
        kvr[g, 2 * TB : KVR, 0:HD] = extra[g]
        for j in range(GH):
            to = slice(j * HD, (j + 1) * HD)
            kvr[g, 0:TB, to] = kin[order_of[g * GH + j]]
            kvr[g, TB : 2 * TB, to] = vin[order_of[g * GH + j]]
        return 0

    def stage_q(g, _):
        for j in range(GH):
            q[g, :, j * HD : (j + 1) * HD] = qin[order_of[g * GH + j]]
        return 0

    sem_wait_bytes(kin, s_l.at[0])
    sem_wait_bytes(vin, s_l.at[1])
    lax.fori_loop(0, 8, stage_kv, 0)

    @pl.when(own)
    def _():
        pltpu.make_async_copy(kvr.at[mine], w2.at[block], r_kv.at[block]).start()
        for n, w in enumerate((wg, wu, wd)):
            pltpu.make_async_copy(w.at[lax.rem(z, 2)], wb.at[n], r_w.at[n]).start()

    @pl.when(row == 0)
    def _():
        w0[...] = jnp.zeros_like(w0)

    @pl.when((row == 0) & (c == 0))
    def _():
        w1[...] = jnp.zeros_like(w1)

    pl.semaphore_wait(barrier, 19 + one(jnp.logical_not(last)) + one(row == 3) + one((row == 0) & (c == 1)) + one(last))

    def target(dz, dx):
        zt, xt = lax.rem(z + dz, 4), lax.rem(x + dx, 2)
        return 4 * xt + zt, dev(row, zt, xt, half)

    @pl.when(jnp.logical_not(own))
    def _():
        rcopy(kvr.at[mine], w2.at[block], s_kv.at[7], r_kv.at[block], partner).start()

    def wave(w):
        for n in WAVES[w]:
            g, to = target(*SEND_ORDER[n])
            rcopy(kvr.at[g], w2.at[block], s_kv.at[n], r_kv.at[block], to).start()

    wave(0)

    @pl.when(own)
    def _():
        for n, w in enumerate((wg, wu, wd)):
            rcopy(w.at[lax.rem(z, 2)], wb.at[n], s_w.at[n], r_w.at[n], partner).start()

    sem_wait_bytes(qin, s_l.at[2])
    lax.fori_loop(0, 8, stage_q, 0)

    @pl.when(own)
    def _():
        pltpu.make_async_copy(q.at[mine], qb.at[block], r_q.at[block]).start()

    for n in range(3):
        sem_wait_bytes(wb.at[n], r_w.at[n])

    def nth(n, local, z_first, x=x):
        p = lax.div(n, 2)
        zs = lax.rem(z_first + jnp.where(local, lax.div(p, 2), lax.rem(lax.div(p + 1, 2), 2)), 2)
        return zs * 4 + lax.rem(x + p, 2) * 2 + lax.rem(n, 2)

    near = jnp.where(own, lax.rem(z, 2), jnp.where(z == 0, 1, jnp.where(z == 3, 0, 1 - lax.rem(z, 2))))

    def arrive(n, _):
        @pl.when(n == 2 * one(own))
        def _():
            for k in WAVES[0]:
                sem_wait_bytes(w2.at[k], s_kv.at[k])
            wave(1)

        b = nth(n, own, near)
        sem_wait_bytes(w2.at[b], r_kv.at[b])
        kv = w2.at[b, pl.ds(0, 2 * TB)]

        direct = jnp.logical_not(last) & ((row != 3) | (n >= 6))

        @pl.when(direct & (c == 0))
        def _():
            rcopy(kv, w0.at[b], s_f.at[b], r_w0.at[b], dev(row + 1, z, x, 0)).start()

        @pl.when(direct & (c == 1))
        def _():
            rcopy(kv, w1.at[b], s_f.at[b], r_w1.at[b], dev(row + 1, z, x, 0)).start()

        @pl.when((row == 3) & (n < 3))
        def _():
            rcopy(kv, rb.at[n], s_f.at[b], r_rb.at[n], dev(0, z, x, c)).start()

        @pl.when((row == 3) & (n >= 3) & (n < 6))
        def _():
            rcopy(kv, rb.at[n - 3], s_f.at[b], r_rb.at[n - 3], dev(7, z, 1 - x, c)).start()

        @pl.when(c == 0)
        def _():
            rcopy(kv, w1.at[b], s_g.at[b], r_w1.at[b], partner).start()

        rows = pl.ds(pl.multiple_of(b * TB, TB), TB)
        k = normed(w2[b, 0:TB, :])
        kn[rows, :] = k
        extra = w2[b, 2 * TB : KVR, 0:HD].astype(F32)
        docs[rows, :] = column(extra[1:2]) * float(TB) + column(extra[2:3])
        rate = column(extra[0:1])
        for j in range(GH):
            at = slice(j * HD, (j + 1) * HD)
            tgt[rows, at] = (rate * w2[b, TB : 2 * TB, at].astype(F32)).astype(BF16)
        pre_gate = dot(k, wb[0], ((1,), (0,)))
        pre_up = dot(k, wb[1], ((1,), (0,)))
        back = -dot(tgt[rows, :], wb[2], ((1,), (1,)))
        sig = jax.nn.sigmoid(pre_gate)
        lifted = pre_gate * sig
        hid[rows, :] = (lifted * pre_up).astype(BF16)
        bgu[rows, 0:FW] = (back * pre_up * sig * (1.0 + pre_gate * (1.0 - sig))).astype(BF16)
        bgu[rows, FW:] = (back * lifted).astype(BF16)
        return 0

    lax.fori_loop(0, 8, arrive, 0)

    @pl.when(carrier)
    def _():
        for m in range(3):
            far = row == 7
            xs = jnp.where(far, 1 - x, x)
            b = nth(m + 3 * one(far), own, near, xs)
            sem_wait_bytes(rb.at[m], r_rb.at[m])

            @pl.when(c == 0)
            def _():
                rcopy(rb.at[m], w0.at[b], s_rb.at[m], r_w0.at[b], dev(4, z, xs, 0)).start()

            @pl.when(c == 1)
            def _():
                rcopy(rb.at[m], w1.at[b], s_rb.at[m], r_w1.at[b], dev(4, z, xs, 0)).start()

    for k in WAVES[1]:
        sem_wait_bytes(w2.at[k], s_kv.at[k])
    def grad_rows(i, _):
        at = pl.ds(pl.multiple_of(i * HD, HD), HD)
        both = dot(kn[:, at], bgu[...], ((0,), (0,)))
        grad[0, at, :] = both[:, 0:FW].astype(BF16)
        grad[1, at, :] = both[:, FW:].astype(BF16)
        grad[2, at, :] = (-dot(hid[:, at], tgt[...], ((0,), (0,)))).astype(BF16)
        return 0

    lax.fori_loop(0, GH, grad_rows, 0)

    rows_of = lambda core, k: pl.ds(pl.multiple_of(core * HALF + peer(k) * PART, 16), PART)
    order = (2, 1, 3, 0)
    for k in order:
        rcopy(grad.at[:, rows_of(1 - c, k), :], r0.at[k], s0.at[k], t0.at[k], partner).start()
    for k in order:
        sem_wait_bytes(r0.at[k], t0.at[k])
        total = grad[:, rows_of(c, k), :].astype(F32) + r0[k].astype(F32)
        if k:
            h[k] = total.astype(BF16)
            rcopy(h.at[k], r1.at[4 - k], s1.at[k], t1.at[4 - k], peer_dev(k)).start()
        else:
            tot[...] = total

    for n, (dz, dx) in enumerate(SEND_ORDER):
        g, to = target(dz, dx)
        rcopy(q.at[g], qb.at[block], s_q.at[n], r_q.at[block], to).start()

    @pl.when(jnp.logical_not(own))
    def _():
        rcopy(q.at[mine], qb.at[block], s_q.at[7], r_q.at[block], partner).start()

    def reduce_y():
        for k in (1, 3, 2):
            sem_wait_bytes(r1.at[k], t1.at[k])
        total = tot[...] + r1[1].astype(F32) + r1[2].astype(F32) + r1[3].astype(F32)
        part[...] = total.astype(BF16)
        rcopy(part, r2, s2, t2, across).start()

    def reduce_x():
        sem_wait_bytes(r2, t2)
        at = rows_of(c, 0)
        gsum[:, at, :] = (part[...].astype(F32) + r2[...].astype(F32)).astype(BF16)
        done = gsum.at[:, at, :]
        for k in (2, 1, 3):
            rcopy(done, done, s3.at[k], t3.at[4 - k], peer_dev(k)).start()
        rcopy(done, done, s4.at[0], t4.at[y], partner).start()

    def reduce_end():
        for k in (1, 3, 2):
            got = gsum.at[:, rows_of(c, k), :]
            sem_wait_bytes(r2, t3.at[k])
            rcopy(got, got, s4.at[k], t4.at[peer(k)], partner).start()
        for k in range(4):
            sem_wait_bytes(r2, t4.at[k])

    reduce_y()

    @pl.when((c == 0) & (row > 0))
    def _():
        def relay(n, _):
            b = nth(n, half == 1, jnp.where(half == 1, lax.rem(z, 2), 1 - z))
            sem_wait_bytes(w1.at[b], r_w1.at[b])
            rcopy(w1.at[b], w0.at[b], s_r.at[b], r_w0.at[b], partner).start()
            return 0

        lax.fori_loop(0, 8, relay, 0)

    @pl.when(row > 0)
    def _():
        for b in range(8):
            sem_wait_bytes(w0.at[b], r_w0.at[b])

    @pl.when(c == 1)
    def _():
        for b in range(8):
            sem_wait_bytes(w1.at[b], r_w1.at[b])

    for b in range(8):
        sem_wait_bytes(qb.at[b], r_q.at[b])

    base = (row * 2048 + c * 1024 - 2048).astype(F32)
    lane = lax.broadcasted_iota(jnp.int32, (TQ, HD), 1).astype(F32)
    down = lax.broadcasted_iota(jnp.int32, (TQ, HD), 0).astype(F32)

    def head(hh, _):
        at = pl.ds(pl.multiple_of(hh * HD, HD), HD)
        win = window[order_of[mine * GH + hh]].astype(F32)
        for n, w in enumerate((w0, w1, w2)):
            for b in range(8):
                rows = slice(n * 1024 + b * TB, n * 1024 + (b + 1) * TB)
                kh[rows, :] = w[b, 0:TB, at]
                vh[rows, :] = w[b, TB : 2 * TB, at]

        def chunk(i, first, width, start):
            keys = pl.ds(first if isinstance(first, int) else pl.multiple_of(first, TQ), width)
            qt = qb[2 * i : 2 * i + 2, :, at].reshape(TQ, HD)
            s = dot(qt, kh[keys, :], ((1,), (1,)))
            off = first.astype(F32) if not isinstance(first, int) else float(first)
            low = jnp.maximum(docs[i * TQ : (i + 1) * TQ, :] - base, down + (2049.0 + TQ * i) - win) - off
            parts = []
            for t in range(width // HD):
                seen = lane >= low - float(HD * t)
                if start:
                    seen = seen & (lane <= down + float(width - TQ - HD * t))
                parts.append(jnp.where(seen, s[:, t * HD : (t + 1) * HD], LOW))
            top = functools.reduce(jnp.maximum, parts)
            top = jnp.broadcast_to(jnp.max(top, axis=1, keepdims=True), (TQ, HD))
            if not start:
                before = ms[i]
                top = jnp.maximum(before, top)
            ms[i] = top
            ps = [jnp.exp2((p - top) * SCALE) for p in parts]
            total = functools.reduce(jnp.add, ps)
            got = dot(jnp.concatenate([p.astype(BF16) for p in ps], axis=1), vh[keys, :], ((1,), (0,)))
            if start:
                ls[i] = total
                accs[i] = got
            else:
                a = jnp.exp2((before - top) * SCALE)
                ls[i] = a * ls[i] + total
                accs[i] = a * accs[i] + got

        for i in range(4):
            chunk(i, 1792 + TQ * i, TK, True)

        def back(r, _):
            for i in range(4):
                chunk(i, 1792 + TQ * i - TK * r, TK, False)
            return 0

        lax.fori_loop(1, 4, back, 0)
        for i in range(4):
            chunk(i, TQ * i, TQ, False)
            att[i * TQ : (i + 1) * TQ, at] = accs[i] / jnp.sum(ls[i], axis=1, keepdims=True)

        @pl.when(hh == 1)
        def _():
            reduce_x()


        return 0

    lax.fori_loop(0, GH, head, 0)
    reduce_end()

    speed = rates[mine]
    for n in range(3):

        def square(i, s):
            g = gsum[n, pl.ds(pl.multiple_of(i * 32, 32), 32), :].astype(F32)
            return s + g * g

        total = lax.fori_loop(0, FW // 32, square, jnp.zeros((32, FW), F32))
        mean = jnp.sum(jnp.sum(total, axis=0, keepdims=True), axis=1, keepdims=True) * (1.0 / (FW * FW))
        factor = speed * lax.rsqrt(mean + 1e-6)

        def move(i, _):
            at = pl.ds(pl.multiple_of(i * HD, HD), HD)
            old = wb[n, :, at].astype(F32)
            moved = old - factor * gsum[n, :, at].astype(F32)
            kept = jnp.sqrt(jnp.sum(old * old, axis=0, keepdims=True))
            fresh = jnp.sqrt(jnp.sum(moved * moved, axis=0, keepdims=True) + 1e-6)
            new[n, :, at] = (moved * (kept / fresh)).astype(BF16)
            return 0

        lax.fori_loop(0, GH, move, 0)

    def tile(n, _):
        b = nth(7 - n, own, near)
        qn = normed(qb[b])
        gate = dot(qn, new[0], ((1,), (0,)))
        up = dot(qn, new[1], ((1,), (0,)))
        applied = (gate * jax.nn.sigmoid(gate) * up).astype(BF16)
        rows = pl.ds(pl.multiple_of(b * TB, TB), TB)
        mixed[b] = (dot(applied, new[2], ((1,), (0,))) + att[rows, :]).astype(BF16)
        zt, xt, ct = 2 * c + lax.div(b, 4), lax.rem(lax.div(b, 2), 2), lax.rem(b, 2)
        here = own & (b == block)

        @pl.when(here)
        def _():
            pltpu.make_async_copy(mixed.at[b], out.at[mine], r_o.at[mine]).start()

        @pl.when(jnp.logical_not(here))
        def _():
            rcopy(mixed.at[b], out.at[mine], s_o.at[b], r_o.at[mine], dev(row, zt, xt, ct)).start()

        return 0

    lax.fori_loop(0, 8, tile, 0)
    for g in range(8):
        sem_wait_bytes(mixed.at[g], r_o.at[g])

    @pl.when(carrier)
    def _():
        for m in range(3):
            sem_wait_bytes(rb.at[m], s_rb.at[m])

    for b in range(8):

        @pl.when(jnp.logical_not(own & (block == b)))
        def _():
            sem_wait_bytes(mixed.at[b], s_o.at[b])

    for n in range(7):
        sem_wait_bytes(qb.at[n], s_q.at[n])

    @pl.when(jnp.logical_not(own))
    def _():
        sem_wait_bytes(w2.at[7], s_kv.at[7])
        sem_wait_bytes(qb.at[7], s_q.at[7])

    @pl.when(own)
    def _():
        for n in range(3):
            sem_wait_bytes(wb.at[n], s_w.at[n])

    @pl.when(c == 0)
    def _():
        for b in range(8):
            sem_wait_bytes(w1.at[b], s_g.at[b])

    @pl.when((c == 0) & (row > 0))
    def _():
        for b in range(8):
            sem_wait_bytes(w1.at[b], s_r.at[b])

    @pl.when(jnp.logical_not(last))
    def _():
        for b in range(8):
            sem_wait_bytes(w1.at[b], s_f.at[b])

    for k in range(4):
        sem_wait_bytes(r2, s0.at[k])
        sem_wait_bytes(r2, s4.at[k])
        if k:
            sem_wait_bytes(r2, s1.at[k])
            sem_wait_bytes(r2, s3.at[k])
    sem_wait_bytes(r2, s2)


def layer(q, k, v, wg, wu, wd, extra, order, rates, window):
    dma = pltpu.SemaphoreType.DMA
    piece = (3, PART, FW)
    mats = (3, FW, FW)
    half = (8 * TB, FW)
    vmem = [
        ((8 * GH, TB, HD), BF16),
        ((8 * GH, TB, HD), BF16),
        ((8 * GH, TB, HD), BF16),
        ((8, KVR, FW), BF16),
        ((8, TB, FW), BF16),
        ((8, KVR, FW), BF16),
        ((8, 2 * TB, FW), BF16),
        ((8, 2 * TB, FW), BF16),
        ((8, TB, FW), BF16),
        (mats, BF16),
        (half, BF16),
        (half, BF16),
        (half, BF16),
        ((8 * TB, 2 * FW), BF16),
        (mats, BF16),
        ((4,) + piece, BF16),
        ((4,) + piece, BF16),
        ((4,) + piece, BF16),
        (piece, F32),
        (piece, BF16),
        (piece, BF16),
        (mats, BF16),
        (mats, BF16),
        ((8 * TB, HD), F32),
        ((3072, HD), BF16),
        ((3072, HD), BF16),
        ((4, TQ, HD), F32),
        ((4, TQ, HD), F32),
        ((4, TQ, HD), F32),
        (half, F32),
        ((8, TB, FW), BF16),
        ((3, 2 * TB, FW), BF16),
    ]
    d4, d8, d3 = dma((4,)), dma((8,)), dma((3,))
    sems = [d3, d8, d8, d8, d8, d8, d3, d8, d8, d8, d8, d3, d4, d4, d4, d4, dma, dma, d4, d4, d4, d4, d8, d8, d3, d3]
    smem = pl.BlockSpec(memory_space=pltpu.SMEM)
    return pl.pallas_call(
        layer_kernel,
        in_specs=[ANY] * 6 + [VM] + [smem] * 3,
        out_specs=ANY,
        out_shape=jax.ShapeDtypeStruct((8, TB, FW), BF16),
        scratch_shapes=[pltpu.VMEM(s, d) for s, d in vmem] + sems,
        compiler_params=pltpu.CompilerParams(
            collective_id=0, has_side_effects=True, vmem_limit_bytes=60 * 1024 * 1024
        ),
        name="layer",
    )(q, k, v, wg, wu, wd, extra, order, rates, window)


def restore_kernel(order, a, o):
    for g in range(8):
        for j in range(GH):
            at = pl.ds(pl.multiple_of(order[g * GH + j] * HD, HD), HD)
            o[:, at] = a[g, :, j * HD : (j + 1) * HD]


def restore(order, a):
    return pl.pallas_call(
        restore_kernel,
        grid_spec=pltpu.PrefetchScalarGridSpec(
            num_scalar_prefetch=1,
            grid=(2,),
            in_specs=[pl.BlockSpec((8, TB // 2, FW), lambda i, o: (0, i, 0))],
            out_specs=pl.BlockSpec((TB // 2, 40 * HD), lambda i, o: (i, 0)),
        ),
        out_shape=jax.ShapeDtypeStruct((TB, 40 * HD), BF16),
        name="restore",
    )(order, a)


def per_device(queries, keys, values, step_rate, doc_start, window_len, head_order, learn_rate, w_gate, w_up, w_down):
    doc = lax.dynamic_slice_in_dim(doc_start, lax.axis_index("head") * TB, TB)
    line = lax.broadcasted_iota(jnp.int32, (8, 16, TB), 1)
    digits = jnp.where(line == 1, (doc // TB)[None, None, :], (doc % TB)[None, None, :]).astype(BF16)
    extra = jnp.where(line == 0, step_rate.T[:, None, :], digits)
    mixed = layer(queries, keys, values, w_gate, w_up, w_down, extra, head_order, learn_rate, window_len)
    return restore(head_order, mixed)


def solution(mesh):
    both = P(("seq", "head"), None)
    placed = (both, both, both, both, P("seq"), P(), P(), P()) + (P("head", None, None),) * 3
    return jax.shard_map(per_device, mesh=mesh, in_specs=placed, out_specs=both, check_vma=False)
```

```python
import functools

import jax
import jax.numpy as jnp
from jax import lax
from jax.experimental import pallas as pl
from jax.experimental.pallas import tpu as pltpu
from jax.sharding import PartitionSpec as P

MESH = pl.DeviceIdType.MESH
ANY = pl.BlockSpec(memory_space=pl.ANY)
VM = pl.BlockSpec(memory_space=pltpu.VMEM)
HD = 128
GH = 5
FW = 640
TB = 128
KVR = 272
ROWS = 8
F32 = jnp.float32
BF16 = jnp.bfloat16

SEND_ORDER = ((0, 1), (1, 0), (3, 0), (2, 1), (1, 1), (2, 0), (3, 1))
WAVES = ((0, 1, 2), (4, 6, 5, 3))


def coords():
    s, h = lax.axis_index("seq"), lax.axis_index("head")
    return lax.div(s, 4), lax.rem(s, 4), lax.div(h, 2), lax.rem(h, 2)


def dev(row, z, x, c):
    return (row * 4 + z, x * 2 + c)


def sem_wait_bytes(ref, sem):
    pltpu.make_async_copy(ref, ref, sem).wait()


def signal(sem, device):
    pl.semaphore_signal(sem, inc=1, device_id=device, device_id_type=MESH)


def rcopy(src, dst, ssem, rsem, device):
    return pltpu.make_async_remote_copy(
        src_ref=src, dst_ref=dst, send_sem=ssem, recv_sem=rsem, device_id=device, device_id_type=MESH
    )


SCALE = HD**-0.5 * 1.4426950408889634
TQ = 256
TK = 512
HALF = FW // 2
PART = FW // 8
LOW = -1e30


def dot(a, b, dims):
    return lax.dot_general(a, b, (dims, ((), ())), preferred_element_type=F32)


def normed(x):
    x = x.astype(F32)
    return (x * lax.rsqrt(jnp.mean(x * x, axis=-1, keepdims=True) + 1e-6)).astype(BF16)


def column(row):
    return jnp.broadcast_to(row, (TB, TB)).T


def layer_kernel(
    qi, ki, vi, wg, wu, wd, extra, order_of, rates, window, out,
    qin, kin, vin, kvr, q, w2, w1, w0, qb, wb, kn, hid, tgt, bgu, grad, r0, h, r1, tot, part, r2, gsum, new, docs, kh, vh, ms, ls, accs, att, mixed, rb,
    s_l, s_kv, s_q, s_f, s_g, s_r, s_w, r_kv, r_q, r_w0, r_w1, r_w, s0, t0, s1, t1, s2, t2, s3, t3, s4, t4, s_o, r_o, s_rb, r_rb,
):
    row, z, x, c = coords()
    half = lax.div(z, 2)
    block = lax.rem(z, 2) * 4 + x * 2 + c
    own = half == c
    mine = 4 * x + z
    y, xh = lax.rem(row, 4), lax.div(row, 4)
    partner = dev(row, z, x, 1 - c)
    across = dev((1 - xh) * 4 + y, z, x, c)
    peer = lambda k: lax.rem(y + k, 4)
    peer_dev = lambda k: dev(xh * 4 + peer(k), z, x, c)
    last = row == ROWS - 1
    one = lambda p: p.astype(jnp.int32)

    for n, (a, b) in enumerate(((ki, kin), (vi, vin), (qi, qin))):

        def fetch(i, _):
            at = pl.ds(pl.multiple_of(i * HD, HD), HD)
            pltpu.make_async_copy(a.at[:, at], b.at[i], s_l.at[n]).start()
            return 0

        lax.fori_loop(0, 8 * GH, fetch, 0)

    barrier = pltpu.get_barrier_semaphore()
    for dz in range(4):
        for dx in range(2):
            for dc in range(2):
                if dz or dx or dc:
                    signal(barrier, dev(row, lax.rem(z + dz, 4), lax.rem(x + dx, 2), lax.rem(c + dc, 2)))
    for k in (1, 2, 3):
        signal(barrier, peer_dev(k))
    signal(barrier, across)

    @pl.when((c == 0) & (row > 0))
    def _():
        signal(barrier, dev(row - 1, z, x, 0))
        signal(barrier, dev(row - 1, z, x, 1))

    @pl.when(row == 7)
    def _():
        signal(barrier, dev(3, z, 1 - x, c))

    @pl.when((row == 4) & (c == 0))
    def _():
        signal(barrier, dev(0, z, x, 1))
        signal(barrier, dev(7, z, 1 - x, 0))
        signal(barrier, dev(7, z, 1 - x, 1))

    carrier = (row == 0) | (row == 7)

    def stage_kv(g, _):
        kvr[g, 2 * TB : KVR, :] = jnp.zeros((KVR - 2 * TB, FW), BF16)
        kvr[g, 2 * TB : KVR, 0:HD] = extra[g]
        for j in range(GH):
            to = slice(j * HD, (j + 1) * HD)
            kvr[g, 0:TB, to] = kin[order_of[g * GH + j]]
            kvr[g, TB : 2 * TB, to] = vin[order_of[g * GH + j]]
        return 0

    def stage_q(g, _):
        for j in range(GH):
            q[g, :, j * HD : (j + 1) * HD] = qin[order_of[g * GH + j]]
        return 0

    sem_wait_bytes(kin, s_l.at[0])
    sem_wait_bytes(vin, s_l.at[1])
    lax.fori_loop(0, 8, stage_kv, 0)

    @pl.when(own)
    def _():
        pltpu.make_async_copy(kvr.at[mine], w2.at[block], r_kv.at[block]).start()
        for n, w in enumerate((wg, wu, wd)):
            pltpu.make_async_copy(w.at[lax.rem(z, 2)], wb.at[n], r_w.at[n]).start()

    @pl.when(row == 0)
    def _():
        w0[...] = jnp.zeros_like(w0)

    @pl.when((row == 0) & (c == 0))
    def _():
        w1[...] = jnp.zeros_like(w1)

    pl.semaphore_wait(barrier, 19 + one(jnp.logical_not(last)) + one(row == 3) + one((row == 0) & (c == 1)) + one(last))

    def target(dz, dx):
        zt, xt = lax.rem(z + dz, 4), lax.rem(x + dx, 2)
        return 4 * xt + zt, dev(row, zt, xt, half)

    @pl.when(jnp.logical_not(own))
    def _():
        rcopy(kvr.at[mine], w2.at[block], s_kv.at[7], r_kv.at[block], partner).start()

    def wave(w):
        for n in WAVES[w]:
            g, to = target(*SEND_ORDER[n])
            rcopy(kvr.at[g], w2.at[block], s_kv.at[n], r_kv.at[block], to).start()

    wave(0)

    @pl.when(own)
    def _():
        for n, w in enumerate((wg, wu, wd)):
            rcopy(w.at[lax.rem(z, 2)], wb.at[n], s_w.at[n], r_w.at[n], partner).start()

    sem_wait_bytes(qin, s_l.at[2])
    lax.fori_loop(0, 8, stage_q, 0)

    @pl.when(own)
    def _():
        pltpu.make_async_copy(q.at[mine], qb.at[block], r_q.at[block]).start()

    for n in range(3):
        sem_wait_bytes(wb.at[n], r_w.at[n])

    def nth(n, local, z_first, x=x):
        p = lax.div(n, 2)
        zs = lax.rem(z_first + jnp.where(local, lax.div(p, 2), lax.rem(lax.div(p + 1, 2), 2)), 2)
        return zs * 4 + lax.rem(x + p, 2) * 2 + lax.rem(n, 2)

    near = jnp.where(own, lax.rem(z, 2), jnp.where(z == 0, 1, jnp.where(z == 3, 0, 1 - lax.rem(z, 2))))

    def arrive(n, _):
        @pl.when(n == 2 * one(own))
        def _():
            for k in WAVES[0]:
                sem_wait_bytes(w2.at[k], s_kv.at[k])
            wave(1)

        b = nth(n, own, near)
        sem_wait_bytes(w2.at[b], r_kv.at[b])
        kv = w2.at[b, pl.ds(0, 2 * TB)]

        direct = jnp.logical_not(last) & ((row != 3) | (n >= 6))

        @pl.when(direct & (c == 0))
        def _():
            rcopy(kv, w0.at[b], s_f.at[b], r_w0.at[b], dev(row + 1, z, x, 0)).start()

        @pl.when(direct & (c == 1))
        def _():
            rcopy(kv, w1.at[b], s_f.at[b], r_w1.at[b], dev(row + 1, z, x, 0)).start()

        @pl.when((row == 3) & (n < 3))
        def _():
            rcopy(kv, rb.at[n], s_f.at[b], r_rb.at[n], dev(0, z, x, c)).start()

        @pl.when((row == 3) & (n >= 3) & (n < 6))
        def _():
            rcopy(kv, rb.at[n - 3], s_f.at[b], r_rb.at[n - 3], dev(7, z, 1 - x, c)).start()

        @pl.when(c == 0)
        def _():
            rcopy(kv, w1.at[b], s_g.at[b], r_w1.at[b], partner).start()

        rows = pl.ds(pl.multiple_of(b * TB, TB), TB)
        k = normed(w2[b, 0:TB, :])
        kn[rows, :] = k
        extra = w2[b, 2 * TB : KVR, 0:HD].astype(F32)
        docs[rows, :] = column(extra[1:2]) * float(TB) + column(extra[2:3])
        rate = column(extra[0:1])
        for j in range(GH):
            at = slice(j * HD, (j + 1) * HD)
            tgt[rows, at] = (rate * w2[b, TB : 2 * TB, at].astype(F32)).astype(BF16)
        pre_gate = dot(k, wb[0], ((1,), (0,)))
        pre_up = dot(k, wb[1], ((1,), (0,)))
        back = -dot(tgt[rows, :], wb[2], ((1,), (1,)))
        sig = jax.nn.sigmoid(pre_gate)
        lifted = pre_gate * sig
        hid[rows, :] = (lifted * pre_up).astype(BF16)
        bgu[rows, 0:FW] = (back * pre_up * sig * (1.0 + pre_gate * (1.0 - sig))).astype(BF16)
        bgu[rows, FW:] = (back * lifted).astype(BF16)
        return 0

    lax.fori_loop(0, 8, arrive, 0)

    @pl.when(carrier)
    def _():
        for m in range(3):
            far = row == 7
            xs = jnp.where(far, 1 - x, x)
            b = nth(m + 3 * one(far), own, near, xs)
            sem_wait_bytes(rb.at[m], r_rb.at[m])

            @pl.when(c == 0)
            def _():
                rcopy(rb.at[m], w0.at[b], s_rb.at[m], r_w0.at[b], dev(4, z, xs, 0)).start()

            @pl.when(c == 1)
            def _():
                rcopy(rb.at[m], w1.at[b], s_rb.at[m], r_w1.at[b], dev(4, z, xs, 0)).start()

    for k in WAVES[1]:
        sem_wait_bytes(w2.at[k], s_kv.at[k])
    def grad_rows(i, _):
        at = pl.ds(pl.multiple_of(i * HD, HD), HD)
        both = dot(kn[:, at], bgu[...], ((0,), (0,)))
        grad[0, at, :] = both[:, 0:FW].astype(BF16)
        grad[1, at, :] = both[:, FW:].astype(BF16)
        grad[2, at, :] = (-dot(hid[:, at], tgt[...], ((0,), (0,)))).astype(BF16)
        return 0

    lax.fori_loop(0, GH, grad_rows, 0)

    rows_of = lambda core, k: pl.ds(pl.multiple_of(core * HALF + peer(k) * PART, 16), PART)
    order = (2, 1, 3, 0)
    for k in order:
        rcopy(grad.at[:, rows_of(1 - c, k), :], r0.at[k], s0.at[k], t0.at[k], partner).start()
    for k in order:
        sem_wait_bytes(r0.at[k], t0.at[k])
        total = grad[:, rows_of(c, k), :].astype(F32) + r0[k].astype(F32)
        if k:
            h[k] = total.astype(BF16)
            rcopy(h.at[k], r1.at[4 - k], s1.at[k], t1.at[4 - k], peer_dev(k)).start()
        else:
            tot[...] = total

    for n, (dz, dx) in enumerate(SEND_ORDER):
        g, to = target(dz, dx)
        rcopy(q.at[g], qb.at[block], s_q.at[n], r_q.at[block], to).start()

    @pl.when(jnp.logical_not(own))
    def _():
        rcopy(q.at[mine], qb.at[block], s_q.at[7], r_q.at[block], partner).start()

    def reduce_y():
        for k in (1, 3, 2):
            sem_wait_bytes(r1.at[k], t1.at[k])
        total = tot[...] + r1[1].astype(F32) + r1[2].astype(F32) + r1[3].astype(F32)
        part[...] = total.astype(BF16)
        rcopy(part, r2, s2, t2, across).start()

    def reduce_x():
        sem_wait_bytes(r2, t2)
        at = rows_of(c, 0)
        gsum[:, at, :] = (part[...].astype(F32) + r2[...].astype(F32)).astype(BF16)
        done = gsum.at[:, at, :]
        for k in (2, 1, 3):
            rcopy(done, done, s3.at[k], t3.at[4 - k], peer_dev(k)).start()
        rcopy(done, done, s4.at[0], t4.at[y], partner).start()

    def reduce_end():
        for k in (1, 3, 2):
            got = gsum.at[:, rows_of(c, k), :]
            sem_wait_bytes(r2, t3.at[k])
            rcopy(got, got, s4.at[k], t4.at[peer(k)], partner).start()
        for k in range(4):
            sem_wait_bytes(r2, t4.at[k])

    reduce_y()

    @pl.when((c == 0) & (row > 0))
    def _():
        def relay(n, _):
            b = nth(n, half == 1, jnp.where(half == 1, lax.rem(z, 2), 1 - z))
            sem_wait_bytes(w1.at[b], r_w1.at[b])
            rcopy(w1.at[b], w0.at[b], s_r.at[b], r_w0.at[b], partner).start()
            return 0

        lax.fori_loop(0, 8, relay, 0)

    @pl.when(row > 0)
    def _():
        for b in range(8):
            sem_wait_bytes(w0.at[b], r_w0.at[b])

    @pl.when(c == 1)
    def _():
        for b in range(8):
            sem_wait_bytes(w1.at[b], r_w1.at[b])

    for b in range(8):
        sem_wait_bytes(qb.at[b], r_q.at[b])

    base = (row * 2048 + c * 1024 - 2048).astype(F32)
    lane = lax.broadcasted_iota(jnp.int32, (TQ, HD), 1).astype(F32)
    down = lax.broadcasted_iota(jnp.int32, (TQ, HD), 0).astype(F32)

    def head(hh, _):
        at = pl.ds(pl.multiple_of(hh * HD, HD), HD)
        win = window[order_of[mine * GH + hh]].astype(F32)
        for n, w in enumerate((w0, w1, w2)):
            for b in range(8):
                rows = slice(n * 1024 + b * TB, n * 1024 + (b + 1) * TB)
                kh[rows, :] = w[b, 0:TB, at]
                vh[rows, :] = w[b, TB : 2 * TB, at]

        def chunk(i, first, width, start):
            keys = pl.ds(first if isinstance(first, int) else pl.multiple_of(first, TQ), width)
            qt = qb[2 * i : 2 * i + 2, :, at].reshape(TQ, HD)
            s = dot(qt, kh[keys, :], ((1,), (1,)))
            off = first.astype(F32) if not isinstance(first, int) else float(first)
            low = jnp.maximum(docs[i * TQ : (i + 1) * TQ, :] - base, down + (2049.0 + TQ * i) - win) - off
            parts = []
            for t in range(width // HD):
                seen = lane >= low - float(HD * t)
                if start:
                    seen = seen & (lane <= down + float(width - TQ - HD * t))
                parts.append(jnp.where(seen, s[:, t * HD : (t + 1) * HD], LOW))
            top = functools.reduce(jnp.maximum, parts)
            top = jnp.broadcast_to(jnp.max(top, axis=1, keepdims=True), (TQ, HD))
            if not start:
                before = ms[i]
                top = jnp.maximum(before, top)
            ms[i] = top
            ps = [jnp.exp2((p - top) * SCALE) for p in parts]
            total = functools.reduce(jnp.add, ps)
            got = dot(jnp.concatenate([p.astype(BF16) for p in ps], axis=1), vh[keys, :], ((1,), (0,)))
            if start:
                ls[i] = total
                accs[i] = got
            else:
                a = jnp.exp2((before - top) * SCALE)
                ls[i] = a * ls[i] + total
                accs[i] = a * accs[i] + got

        for i in range(4):
            chunk(i, 1792 + TQ * i, TK, True)

        def back(r, _):
            for i in range(4):
                chunk(i, 1792 + TQ * i - TK * r, TK, False)
            return 0

        lax.fori_loop(1, 4, back, 0, unroll=True)
        for i in range(4):
            chunk(i, TQ * i, TQ, False)
            att[i * TQ : (i + 1) * TQ, at] = accs[i] / jnp.sum(ls[i], axis=1, keepdims=True)

        @pl.when(hh == 0)
        def _():
            reduce_x()


        return 0

    lax.fori_loop(0, GH, head, 0)
    reduce_end()

    speed = rates[mine]
    for n in range(3):

        def square(i, s):
            g = gsum[n, pl.ds(pl.multiple_of(i * 32, 32), 32), :].astype(F32)
            return s + g * g

        total = lax.fori_loop(0, FW // 32, square, jnp.zeros((32, FW), F32))
        mean = jnp.sum(jnp.sum(total, axis=0, keepdims=True), axis=1, keepdims=True) * (1.0 / (FW * FW))
        factor = speed * lax.rsqrt(mean + 1e-6)

        def move(i, _):
            at = pl.ds(pl.multiple_of(i * HD, HD), HD)
            old = wb[n, :, at].astype(F32)
            moved = old - factor * gsum[n, :, at].astype(F32)
            kept = jnp.sqrt(jnp.sum(old * old, axis=0, keepdims=True))
            fresh = jnp.sqrt(jnp.sum(moved * moved, axis=0, keepdims=True) + 1e-6)
            new[n, :, at] = (moved * (kept / fresh)).astype(BF16)
            return 0

        lax.fori_loop(0, GH, move, 0)

    def tile(n, _):
        b = nth(7 - n, own, near)
        qn = normed(qb[b])
        gate = dot(qn, new[0], ((1,), (0,)))
        up = dot(qn, new[1], ((1,), (0,)))
        applied = (gate * jax.nn.sigmoid(gate) * up).astype(BF16)
        rows = pl.ds(pl.multiple_of(b * TB, TB), TB)
        mixed[b] = (dot(applied, new[2], ((1,), (0,))) + att[rows, :]).astype(BF16)
        zt, xt, ct = 2 * c + lax.div(b, 4), lax.rem(lax.div(b, 2), 2), lax.rem(b, 2)
        here = own & (b == block)

        @pl.when(here)
        def _():
            pltpu.make_async_copy(mixed.at[b], out.at[mine], r_o.at[mine]).start()

        @pl.when(jnp.logical_not(here))
        def _():
            rcopy(mixed.at[b], out.at[mine], s_o.at[b], r_o.at[mine], dev(row, zt, xt, ct)).start()

        return 0

    lax.fori_loop(0, 8, tile, 0)
    for g in range(8):
        sem_wait_bytes(mixed.at[g], r_o.at[g])

    @pl.when(carrier)
    def _():
        for m in range(3):
            sem_wait_bytes(rb.at[m], s_rb.at[m])

    for b in range(8):

        @pl.when(jnp.logical_not(own & (block == b)))
        def _():
            sem_wait_bytes(mixed.at[b], s_o.at[b])

    for n in range(7):
        sem_wait_bytes(qb.at[n], s_q.at[n])

    @pl.when(jnp.logical_not(own))
    def _():
        sem_wait_bytes(w2.at[7], s_kv.at[7])
        sem_wait_bytes(qb.at[7], s_q.at[7])

    @pl.when(own)
    def _():
        for n in range(3):
            sem_wait_bytes(wb.at[n], s_w.at[n])

    @pl.when(c == 0)
    def _():
        for b in range(8):
            sem_wait_bytes(w1.at[b], s_g.at[b])

    @pl.when((c == 0) & (row > 0))
    def _():
        for b in range(8):
            sem_wait_bytes(w1.at[b], s_r.at[b])

    @pl.when(jnp.logical_not(last))
    def _():
        for b in range(8):
            sem_wait_bytes(w1.at[b], s_f.at[b])

    for k in range(4):
        sem_wait_bytes(r2, s0.at[k])
        sem_wait_bytes(r2, s4.at[k])
        if k:
            sem_wait_bytes(r2, s1.at[k])
            sem_wait_bytes(r2, s3.at[k])
    sem_wait_bytes(r2, s2)


def layer(q, k, v, wg, wu, wd, extra, order, rates, window):
    dma = pltpu.SemaphoreType.DMA
    piece = (3, PART, FW)
    mats = (3, FW, FW)
    half = (8 * TB, FW)
    vmem = [
        ((8 * GH, TB, HD), BF16),
        ((8 * GH, TB, HD), BF16),
        ((8 * GH, TB, HD), BF16),
        ((8, KVR, FW), BF16),
        ((8, TB, FW), BF16),
        ((8, KVR, FW), BF16),
        ((8, 2 * TB, FW), BF16),
        ((8, 2 * TB, FW), BF16),
        ((8, TB, FW), BF16),
        (mats, BF16),
        (half, BF16),
        (half, BF16),
        (half, BF16),
        ((8 * TB, 2 * FW), BF16),
        (mats, BF16),
        ((4,) + piece, BF16),
        ((4,) + piece, BF16),
        ((4,) + piece, BF16),
        (piece, F32),
        (piece, BF16),
        (piece, BF16),
        (mats, BF16),
        (mats, BF16),
        ((8 * TB, HD), F32),
        ((3072, HD), BF16),
        ((3072, HD), BF16),
        ((4, TQ, HD), F32),
        ((4, TQ, HD), F32),
        ((4, TQ, HD), F32),
        (half, F32),
        ((8, TB, FW), BF16),
        ((3, 2 * TB, FW), BF16),
    ]
    d4, d8, d3 = dma((4,)), dma((8,)), dma((3,))
    sems = [d3, d8, d8, d8, d8, d8, d3, d8, d8, d8, d8, d3, d4, d4, d4, d4, dma, dma, d4, d4, d4, d4, d8, d8, d3, d3]
    smem = pl.BlockSpec(memory_space=pltpu.SMEM)
    return pl.pallas_call(
        layer_kernel,
        in_specs=[ANY] * 6 + [VM] + [smem] * 3,
        out_specs=ANY,
        out_shape=jax.ShapeDtypeStruct((8, TB, FW), BF16),
        scratch_shapes=[pltpu.VMEM(s, d) for s, d in vmem] + sems,
        compiler_params=pltpu.CompilerParams(
            collective_id=0, has_side_effects=True, vmem_limit_bytes=60 * 1024 * 1024
        ),
        name="layer",
    )(q, k, v, wg, wu, wd, extra, order, rates, window)


def restore_kernel(order, a, o):
    for g in range(8):
        for j in range(GH):
            at = pl.ds(pl.multiple_of(order[g * GH + j] * HD, HD), HD)
            o[:, at] = a[g, :, j * HD : (j + 1) * HD]


def restore(order, a):
    return pl.pallas_call(
        restore_kernel,
        grid_spec=pltpu.PrefetchScalarGridSpec(
            num_scalar_prefetch=1,
            grid=(2,),
            in_specs=[pl.BlockSpec((8, TB // 2, FW), lambda i, o: (0, i, 0))],
            out_specs=pl.BlockSpec((TB // 2, 40 * HD), lambda i, o: (i, 0)),
        ),
        out_shape=jax.ShapeDtypeStruct((TB, 40 * HD), BF16),
        name="restore",
    )(order, a)


def per_device(queries, keys, values, step_rate, doc_start, window_len, head_order, learn_rate, w_gate, w_up, w_down):
    doc = lax.dynamic_slice_in_dim(doc_start, lax.axis_index("head") * TB, TB)
    line = lax.broadcasted_iota(jnp.int32, (8, 16, TB), 1)
    digits = jnp.where(line == 1, (doc // TB)[None, None, :], (doc % TB)[None, None, :]).astype(BF16)
    extra = jnp.where(line == 0, step_rate.T[:, None, :], digits)
    mixed = layer(queries, keys, values, w_gate, w_up, w_down, extra, head_order, learn_rate, window_len)
    return restore(head_order, mixed)


def solution(mesh):
    both = P(("seq", "head"), None)
    placed = (both, both, both, both, P("seq"), P(), P(), P()) + (P("head", None, None),) * 3
    return jax.shard_map(per_device, mesh=mesh, in_specs=placed, out_specs=both, check_vma=False)
```
